32 devices in a mesh: server: 16 (over z, x, core), helper: 2 (over y).
Axes of the slice: x: 2, y: 2, z: 4, core: 2. Of those that a mesh axis runs over, the one named last changes fastest.
Arguments:
- hidden_in: bfloat16 [512, 4, 4096], P('server', None, 'helper'), may hold values from -6 to 6
- base_out: bfloat16 [512, 4, 4096], P('server', None, 'helper'), may hold values from -6 to 6
- adapter_ids: int32 [512], P('server'), may hold values from 0 to 383, as said below
- left_blocks: bfloat16 [384, 64, 4096], P('server', 'helper'), may hold values from -0.75 to 0.75
- right_blocks: bfloat16 [384, 64, 4096], P('server', 'helper'), may hold values from -0.75 to 0.75
- down_rank: bfloat16 [384, 4096, 16], P('server', 'helper'), may hold values from -0.09375 to 0.09375
- up_rank: bfloat16 [384, 16, 4096], P('server', None, 'helper'), may hold values from -1.5 to 1.5
Outputs:
- adapted: bfloat16 [512, 4, 4096], P('server', None, 'helper')
The draws below stay inside these ranges and needn't reach their ends.
Inputs may be any that keep to these rules, and one draw needn't show every extreme that they name: `adapter_ids`: of the requests of one server group (aligned blocks of 32), at most 2 name adapters of one owner, the owner of adapter a being a // 24; in every draw some owner gets exactly 2 from every group.
All inputs are finite; a program needn't handle non-finite values.
Results may differ from the reference program's by a relative error of at most 0.0059.
Values may be sent and summed in bfloat16 or wider, within the bound.
A program may use at most 64 MiB of HBM per device.

```python
import jax
import jax.numpy as jnp
from jax import lax

D = 4096
BLOCK = 64
RANK = 16
POS = 4
ADP_SRV = 24
CAP = 2
REQ_SRV = 32
ADAPTERS = 384
REQS = 512


def draw_adapter_ids(key, part):
    groups = REQS // REQ_SRV
    slot_count = groups * CAP
    subkeys = jax.random.split(key, 5)
    warmth = jax.random.randint(subkeys[0], (groups,), 0, 4) * 16384
    favored = jax.random.randint(subkeys[1], (), 0, groups)
    warmth = jnp.where(jnp.arange(groups) == favored, 1 << 20, warmth)
    slot_warmth = jnp.repeat(warmth, CAP)
    jitter = jax.random.randint(subkeys[2], (groups, slot_count), 0, 65536)
    scores = (slot_warmth[None, :] + jitter) * slot_count + jnp.arange(slot_count)[None, :]
    chosen = lax.top_k(scores, REQ_SRV)[1]
    shuffle_keys = jax.random.randint(subkeys[3], (groups, REQ_SRV), 0, 1 << 20) * REQ_SRV + jnp.arange(REQ_SRV)[None, :]
    shuffle = jnp.argsort(shuffle_keys, axis=1)
    chosen = jnp.take_along_axis(chosen, shuffle, axis=1)
    owners = chosen // CAP
    local_id = jax.random.randint(subkeys[4], (groups, REQ_SRV), 0, ADP_SRV)
    return (owners * ADP_SRV + local_id).reshape(REQS).astype(jnp.int32)


def block_levels(own_key, extent, cuts, low, top_value):
    def one(dim, parts):
        heights = jax.random.uniform(jax.random.fold_in(jax.random.fold_in(own_key, 6), dim), (parts,), jnp.float32, low / len(cuts), top_value / len(cuts))
        return jnp.repeat(jnp.exp(heights), extent[dim] // parts).reshape((-1,) + (1,) * (len(extent) - dim - 1))

    level = one(*cuts[0])
    for cut in cuts[1:]:
        level = level * one(*cut)
    return level


def bell_draw(rng, shape, scale, bound, cuts=(), held_as=jnp.bfloat16):
    result = jax.random.normal(rng, shape, jnp.float32) * scale
    if len(cuts) > 0:
        result = block_levels(rng, shape, cuts, -0.22, 0.18) * result
    return jnp.clip(result, min=-bound, max=bound).astype(held_as)


def setup_inputs(seed: int = 0) -> dict:
    streams_of = jax.random.split(jax.random.key(seed), 8)
    return {
        "hidden_in": bell_draw(streams_of[0], (REQS, POS, D), 1.0, 6.0, ((0, 16), (2, 2))),
        "base_out": bell_draw(streams_of[1], (REQS, POS, D), 1.0, 6.0, ((0, 16), (2, 2))),
        "adapter_ids": draw_adapter_ids(jax.random.fold_in(streams_of[7], 71), 0),
        "left_blocks": bell_draw(streams_of[3], (ADAPTERS, BLOCK, D), BLOCK ** -0.5, 0.75, ((0, 16), (1, 2))),
        "right_blocks": bell_draw(streams_of[4], (ADAPTERS, BLOCK, D), BLOCK ** -0.5, 0.75, ((0, 16), (1, 2))),
        "down_rank": bell_draw(streams_of[5], (ADAPTERS, D, RANK), D ** -0.5, 0.09375, ((0, 16), (1, 2))),
        "up_rank": bell_draw(streams_of[6], (ADAPTERS, RANK, D), RANK ** -0.5, 1.5, ((0, 16), (2, 2))),
    }


def reference(hidden_in, base_out, adapter_ids, left_blocks, right_blocks, down_rank, up_rank):
    def one_request(inputs):
        features, base_rows, adapter = inputs
        left_tile = left_blocks[adapter].astype(jnp.float32).reshape(BLOCK, BLOCK, BLOCK)
        right_tile = right_blocks[adapter].astype(jnp.float32).reshape(BLOCK, BLOCK, BLOCK)
        blocks_in = features.astype(jnp.float32).reshape(POS, BLOCK, BLOCK)
        mixed = jnp.einsum("pij,ikj->pik", blocks_in, left_tile, precision=lax.Precision.HIGHEST).astype(jnp.bfloat16)
        mixed = lax.optimization_barrier(mixed).astype(jnp.float32)
        right_out = jnp.einsum("pik,kmi->pmk", mixed, right_tile, precision=lax.Precision.HIGHEST).astype(jnp.bfloat16)
        monarch = right_out.reshape(POS, D)
        rank_proj = jnp.dot(features, down_rank[adapter], preferred_element_type=jnp.float32).astype(jnp.bfloat16)
        rank_out = jnp.dot(rank_proj, up_rank[adapter], preferred_element_type=jnp.float32).astype(jnp.bfloat16)
        delta = (monarch.astype(jnp.float32) + rank_out.astype(jnp.float32)).astype(jnp.bfloat16)
        total = base_rows.astype(jnp.float32) + delta.astype(jnp.float32)
        return total.astype(jnp.bfloat16)

    return lax.map(one_request, (hidden_in, base_out, adapter_ids))
```

```python
import functools

import jax
import jax.numpy as jnp
from jax import lax
from jax.experimental import pallas as pl
from jax.experimental.pallas import tpu as pltpu
from jax.sharding import PartitionSpec as P

BLOCK = 64
CAP = 2


def plain(hidden_in, base_out, adapter_ids, left_blocks, right_blocks, down_rank, up_rank):
    servers = lax.axis_size("server")
    requests, positions, width_here = hidden_in.shape
    adapters_here = left_blocks.shape[0]
    blocks_here = left_blocks.shape[1]
    block_size = BLOCK
    rank_width = down_rank.shape[2]
    slot_total = servers * CAP
    owners = adapter_ids // adapters_here
    local_id = adapter_ids % adapters_here
    number = jnp.arange(requests)
    earlier = (owners[:, None] == owners[None, :]) & (number[None, :] < number[:, None])
    target = owners * CAP + jnp.sum(earlier.astype(jnp.int32), axis=1)
    placing = (jnp.arange(slot_total)[:, None] == target[None, :]).astype(jnp.bfloat16)
    packed = jnp.dot(
        placing,
        hidden_in.reshape(requests, positions * width_here),
        preferred_element_type=jnp.float32,
    ).astype(jnp.bfloat16)
    labels = jnp.dot(
        placing, (local_id + 1).astype(jnp.bfloat16), preferred_element_type=jnp.float32
    ).astype(jnp.bfloat16)
    arrived, arrived_labels = (
        lax.all_to_all(
            packed.reshape(servers, CAP, positions, width_here),
            "server",
            split_axis=0,
            concat_axis=0,
            tiled=True,
        ),
        lax.all_to_all(
            labels.reshape(servers, CAP), "server", split_axis=0, concat_axis=0, tiled=True
        ),
    )
    row_count = slot_total * positions
    flat_rows = arrived.reshape(row_count, width_here)
    block_rows = arrived.reshape(row_count, blocks_here, block_size)
    slot_labels = arrived_labels.reshape(slot_total, 1).astype(jnp.int32)
    row_labels = jnp.broadcast_to(slot_labels, (slot_total, positions)).reshape(row_count)
    numbers = jnp.arange(adapters_here, dtype=jnp.int32)

    def first_factor(carry, inputs):
        mixed_acc, rank_acc = carry
        left_flat, down_tile, number = inputs
        left_tile = left_flat.reshape(blocks_here, block_size, block_size)
        selected = row_labels == number + 1
        mixed = jnp.einsum(
            "rij,ikj->rik", block_rows, left_tile, preferred_element_type=jnp.float32
        ).astype(jnp.bfloat16)
        mixed_acc = jnp.where(selected[:, None, None], mixed, mixed_acc)
        partial_rank = jnp.dot(flat_rows, down_tile, preferred_element_type=jnp.float32)
        rank_acc = jnp.where(selected[:, None], partial_rank, rank_acc)
        return ((mixed_acc, rank_acc), None)

    start_mixed = jnp.zeros((row_count, blocks_here, block_size), jnp.bfloat16)
    start_rank = jnp.zeros((row_count, rank_width), jnp.float32)
    (mixed_rows, rank_partial), ignored = lax.scan(
        first_factor, (start_mixed, start_rank), (left_blocks, down_rank, numbers)
    )
    turned = lax.all_to_all(mixed_rows, "helper", split_axis=2, concat_axis=1, tiled=True)
    rank_sum = lax.psum(rank_partial, "helper")
    rank_proj = rank_sum.astype(jnp.bfloat16)
    columns_here = turned.shape[2]

    def second_factor(carry, inputs):
        right_acc, low_acc = carry
        right_flat, up_tile, number = inputs
        right_tile = right_flat.reshape(right_flat.shape[0], block_size, block_size)
        selected = row_labels == number + 1
        right_out = jnp.einsum(
            "rik,kmi->rmk", turned, right_tile, preferred_element_type=jnp.float32
        ).astype(jnp.bfloat16)
        right_acc = jnp.where(selected[:, None, None], right_out, right_acc)
        low_out = jnp.dot(rank_proj, up_tile, preferred_element_type=jnp.float32).astype(
            jnp.bfloat16
        )
        low_acc = jnp.where(selected[:, None], low_out, low_acc)
        return ((right_acc, low_acc), None)

    start_right = jnp.zeros((row_count, block_size, columns_here), jnp.bfloat16)
    start_low = jnp.zeros((row_count, width_here), jnp.bfloat16)
    (right_rows, rank_rows), ignored = lax.scan(
        second_factor, (start_right, start_low), (right_blocks, up_rank, numbers)
    )
    monarch_rows = lax.all_to_all(
        right_rows, "helper", split_axis=1, concat_axis=2, tiled=True
    ).reshape(row_count, width_here)
    summed_rows = (monarch_rows.astype(jnp.float32) + rank_rows.astype(jnp.float32)).astype(
        jnp.bfloat16
    )
    back_delta = lax.all_to_all(
        summed_rows.reshape(servers, CAP, positions, width_here),
        "server",
        split_axis=0,
        concat_axis=0,
        tiled=True,
    )
    flat_buffer = back_delta.reshape(slot_total, -1)
    delta = (
        jnp.einsum("sr,sc->rc", placing, flat_buffer, preferred_element_type=jnp.float32)
        .astype(jnp.bfloat16)
        .reshape(requests, positions, width_here)
    )
    total = base_out.astype(jnp.float32) + delta.astype(jnp.float32)
    return total.astype(jnp.bfloat16)


LANES = 128
SUB = 8
SPAN = 2
VMEM_LIMIT = 56 << 20
PARTS = 4
DEPTH = 2
MESH = pl.DeviceIdType.MESH
NT = (((1,), (1,)), ((), ()))
BF = jnp.bfloat16
F32 = jnp.float32
I32 = jnp.int32


def iota(shape, dim=1):
    return lax.broadcasted_iota(I32, shape, dim)


def flipped(index, mask):
    other = index
    bit = 1
    while bit <= mask:
        if mask & bit:
            other = other + bit * (1 - 2 * lax.rem(lax.div(index, bit), 2))
        bit *= 2
    return other


def flipped_by(index, mask, count):
    other = index
    bit = 1
    while bit < count:
        has = lax.rem(lax.div(mask, bit), 2)
        other = other + bit * has * (1 - 2 * lax.rem(lax.div(index, bit), 2))
        bit *= 2
    return other


def order_of(i, chunks):
    half = chunks // 2
    near, far = list(range(half)), list(range(half, chunks))
    listed = near[:2]
    rest = near[2:]
    for c in far:
        listed.append(c)
        if rest:
            listed.append(rest.pop(0))
    chunk = jnp.int32(0)
    for at, c in enumerate(listed):
        chunk = chunk + jnp.where(i == at, c, 0).astype(I32)
    return chunk


def expand(x):
    low = iota(x.shape) < LANES // 2
    zero = jnp.zeros_like(x)
    turned = pltpu.roll(x, LANES // 2, 1)
    both = jnp.concatenate(
        [
            jnp.where(low, x, zero),
            jnp.where(low, turned, zero),
            jnp.where(low, zero, turned),
            jnp.where(low, zero, x),
        ],
        axis=0,
    ).astype(BF)
    none = jnp.zeros_like(both)
    return jnp.concatenate(
        [jnp.concatenate([both, none], axis=1), jnp.concatenate([none, both], axis=1)], axis=0
    )


def diagonal(full, number):
    wide = full.shape[1]
    groups = full.shape[0] // (2 * SUB)
    sub = iota((SUB, wide), 0)
    parts = full.reshape(groups, 2, SUB, wide)
    upper = number >= SUB
    sets = []
    for h in range(groups // SUB):
        held = [
            jnp.where(upper, parts[h * SUB + c, 1], parts[h * SUB + c, 0]) for c in range(SUB)
        ]
        for bit in (4, 2, 1):
            here = (sub & bit) > 0
            same = ((number & bit) > 0) == here
            merged = []
            for c in range(bit):
                a, b = held[c], held[c + bit]
                kept = jnp.where(here, b, a)
                moved = jnp.where(here, a, b)
                if 2 * bit == SUB:
                    moved = pltpu.roll(moved, bit, 0)
                else:
                    moved = jnp.where(
                        here, pltpu.roll(moved, bit, 0), pltpu.roll(moved, SUB - bit, 0)
                    )
                merged.append(jnp.where(same, kept, moved))
            held = merged
        sets.append(held[0])
    return sets


def factor(w, which, groups, number, wide):
    chunks = w.shape[2] // wide
    sets = []
    for g, x in enumerate(groups):
        rows = jnp.concatenate(
            [
                w[which, 2 * SUB * g : 2 * SUB * (g + 1), c * wide : (c + 1) * wide]
                for c in range(chunks)
            ],
            axis=0,
        )
        full = lax.dot_general(rows, expand(x), NT, preferred_element_type=F32)
        sets.append(diagonal(full, number))
    return jnp.concatenate([sets[g][h] for h in range(2) for g in range(2)], axis=0)


def exchanged(pieces):
    lane = iota((SUB, LANES))
    first, second = (lane & 16) > 0, (lane & 32) > 0
    result = [[None, None] for _ in range(4)]
    for high in range(2):
        at = slice(high * LANES, (high + 1) * LANES)
        by_g = []
        for h in range(2):
            a, b = pieces[h][0][:, at], pieces[h][1][:, at]
            by_g.append(
                (
                    jnp.where(first, pltpu.roll(b, 16, 1), a),
                    jnp.where(first, b, pltpu.roll(a, LANES - 16, 1)),
                )
            )
        for p0 in range(2):
            a, b = by_g[0][p0], by_g[1][p0]
            result[p0][high] = jnp.where(second, pltpu.roll(b, 32, 1), a)
            result[2 + p0][high] = jnp.where(second, b, pltpu.roll(a, LANES - 32, 1))
    return result


def halves(ref, slot):
    found = []
    for h in range(2):
        both = ref[h, slot].astype(F32)
        found.append((both[:SUB], both[SUB:]))
    return found


def stacked(ref, at, width):
    return jnp.concatenate(
        [ref[at, :, k * LANES : (k + 1) * LANES] for k in range(width // LANES)], axis=0
    )


def fused_kernel(
    helpers, count, adapters,
    ids_any, hid_any, base_any, left_any, right_any, down_any, up_any,
    back, base, table_s,
    left, right, down, up, ids, hid, packed, arrived, table, lab, lab_in, lab_s,
    mixed, got1, rank, got_rank, right_out, got2, low, delta, order_m, perm1, perm2,
    wsem, isem, tsem, lsem, send, recv, lsend, lrecv, s1, r1, s2, r2, s3, r3, bsend, brecv,
):
    me = lax.axis_index("helper")
    here = lax.axis_index("server")
    other = 1 - me
    slots, rows, _ = packed.shape
    wide = mixed.shape[2]
    positions = 4
    tiles = rows // positions
    cap = slots // count
    chunks = count // SPAN
    size = SPAN * cap
    requests = ids.shape[1]

    barrier = pltpu.get_barrier_semaphore()
    for step in range(1, count):
        pl.semaphore_signal(
            barrier, inc=1, device_id={"server": flipped(here, step)}, device_id_type=MESH
        )
    pl.semaphore_signal(barrier, inc=1, device_id={"helper": other}, device_id_type=MESH)
    load_ids = pltpu.make_async_copy(ids_any, ids, isem.at[0])
    load_ids.start()
    load_hid = pltpu.make_async_copy(hid_any, hid, isem.at[1])
    load_hid.start()
    loads = [
        pltpu.make_async_copy(a, b, wsem.at[i])
        for i, (a, b) in enumerate(
            ((left_any, left), (down_any, down), (right_any, right), (up_any, up))
        )
    ]
    for load in loads:
        load.start()
    load_base = pltpu.make_async_copy(base_any, base, isem.at[2])
    load_base.start()

    load_ids.wait()
    names = ids[...]
    owner = jnp.zeros_like(names)
    for s in range(1, count):
        owner = owner + (names >= s * adapters).astype(I32)
    local = names - owner * adapters
    lane = iota((requests, requests))
    row = iota((requests, requests), 0)

    def column(line):
        return jnp.sum(jnp.where(lane == row, line, 0), axis=1, keepdims=True)

    owner_column = column(owner)
    same_owner = owner_column == owner
    before_line = jnp.sum((same_owner & (row < lane)).astype(I32), axis=0, keepdims=True)
    target_line = (owner ^ here) * cap + before_line
    target_column = column(target_line)
    slot_lane = iota((requests, LANES))
    hit = target_column == slot_lane
    inv_line = jnp.sum(jnp.where(hit, iota((requests, LANES), 0), 0), axis=0, keepdims=True)
    table[...] = jnp.zeros_like(table)
    table[0:1, :] = inv_line
    table[1:2, 0:requests] = target_line
    save = pltpu.make_async_copy(table, table_s, tsem.at[0])
    save.start()
    step_row = iota((count, requests), 0)
    step_line = owner ^ here
    lab_lane = iota((count, LANES))
    labels = jnp.zeros((count, LANES), I32)
    for u in range(cap):
        mine = (step_line == step_row) & (before_line == u)
        found = jnp.sum(jnp.where(mine, local, 0), axis=1, keepdims=True)
        labels = labels + jnp.where(lab_lane == u, found, 0)
    for step in range(count):
        lab[step] = labels[step : step + 1]
    lab_in[0] = labels[0:1]
    save.wait()
    load_hid.wait()
    for s in range(slots):
        packed[s] = hid[table_s[0, s]].astype(F32).reshape(rows, LANES).astype(BF)
    pl.semaphore_wait(barrier, count)

    def lab_copy(step):
        return pltpu.make_async_remote_copy(
            src_ref=lab.at[step], dst_ref=lab_in.at[step],
            send_sem=lsend.at[step], recv_sem=lrecv.at[step],
            device_id={"server": flipped_by(here, step, count)}, device_id_type=MESH,
        )

    def data_copy(step):
        at = pl.ds(step * cap, cap)
        return pltpu.make_async_remote_copy(
            src_ref=packed.at[at], dst_ref=arrived.at[at],
            send_sem=send.at[step], recv_sem=recv.at[step],
            device_id={"server": flipped_by(here, step, count)}, device_id_type=MESH,
        )

    def back_copy(step):
        at = pl.ds(step * cap, cap)
        return pltpu.make_async_remote_copy(
            src_ref=delta.at[at], dst_ref=back.at[at],
            send_sem=bsend.at[step], recv_sem=brecv.at[step],
            device_id={"server": flipped_by(here, step, count)}, device_id_type=MESH,
        )

    def to_helper(c, src, dst, s, r, scale=1):
        at = pl.ds(c * (size // scale), size // scale)
        return pltpu.make_async_remote_copy(
            src_ref=src.at[at], dst_ref=dst.at[me, at],
            send_sem=s.at[c], recv_sem=r.at[c],
            device_id={"helper": other}, device_id_type=MESH,
        )

    for step in range(1, count):
        lab_copy(step).start()
    issue = [s + j for j in range(count // 4) for s in (count // 2, 3 * (count // 4))]
    issue += list(range(1, count // 2))
    for step in issue:
        data_copy(step).start()
    own = pl.ds(0, cap)
    arrived[own] = packed[own]

    src = iota((wide, wide), 0)
    dst = iota((wide, wide))
    q, low32, par = src & 192, src & 31, (src >> 5) & 1
    perm1[...] = (
        (q + (low32 & 3) * 16 + 2 * (low32 >> 2) + par == dst).astype(F32).astype(BF)
    )
    perm2[...] = (
        (q + (low32 >> 3) * 16 + 4 * (low32 & 3) + (low32 & 4) // 2 + par == dst)
        .astype(F32)
        .astype(BF)
    )
    code = iota((SUB, wide))
    low32, par = code & 31, (code >> 5) & 1
    number1 = 2 * (low32 >> 2) + par
    number2 = 4 * (low32 & 3) + (low32 & 4) // 2 + par
    sub = iota((SUB, LANES), 0)
    line = iota((SUB, LANES))
    top = sub < positions
    rank_width = LANES // SUB
    nothing = jnp.zeros((SUB, LANES), F32)

    def diag_of(b):
        return line // rank_width == 2 * (b % (tiles // 4)) + sub // positions

    def first(c):
        pieces, ranks = [], []
        for j in range(size):
            slot = c * size + j
            which = lab_s[c * SPAN + j // cap, 0, j % cap]
            x = arrived[slot]
            xf = x.astype(F32)
            pieces.append(factor(left, which, [xf[: rows // 2], xf[rows // 2 :]], number1, wide))
            part = lax.dot_general(
                x, stacked(down, which, tiles * LANES), NT, preferred_element_type=F32
            )
            total = None
            for b in range(rows // SUB):
                half = b // (tiles // 4)
                block = part[b * SUB : (b + 1) * SUB, half * LANES : (half + 1) * LANES]
                block = jnp.where(diag_of(b), block, 0.0)
                total = block if total is None else total + block
            ranks.append(total + pltpu.roll(total, positions, 0))
        turned = jnp.dot(
            jnp.concatenate(pieces, axis=0).astype(BF), perm1[...], preferred_element_type=F32
        ).astype(BF)
        for j in range(size):
            slot = c * size + j
            a = turned[j * 2 * tiles : j * 2 * tiles + tiles]
            b = turned[j * 2 * tiles + tiles : (j + 1) * 2 * tiles]
            got1[me, slot] = jnp.where(me == 0, a, b)
            mixed[slot] = jnp.where(me == 0, b, a)
        for k in range(size // 2):
            pair = c * (size // 2) + k
            both = jnp.where(top, ranks[2 * k], ranks[2 * k + 1])
            rank[pair] = both
            got_rank[me, pair] = both

    def second(c):
        pieces = []
        for k in range(size // 2):
            pair = c * (size // 2) + k
            total = got_rank[0, pair] + got_rank[1, pair]
            for shift in (64, 32, 16):
                total = total + pltpu.roll(total, shift, 1)
            total = total.astype(BF).astype(F32)
            swapped = pltpu.roll(total, positions, 0)
            for u in range(2):
                slot = c * size + 2 * k + u
                which = lab_s[c * SPAN + (2 * k + u) // cap, 0, (2 * k + u) % cap]
                held = exchanged(halves(got1, slot))
                groups = []
                for g in range(2):
                    blocks = []
                    for p in range(positions):
                        a, b = held[p]
                        if g == 0:
                            blocks.append(jnp.where(top, a, pltpu.roll(b, positions, 0)))
                        else:
                            blocks.append(jnp.where(top, pltpu.roll(a, positions, 0), b))
                    groups.append(jnp.concatenate(blocks, axis=0))
                pieces.append(factor(right, which, groups, number2, wide))
                mine = jnp.where(top, total, swapped) if u == 0 else jnp.where(top, swapped, total)
                blocks = []
                for b in range(rows // SUB):
                    kept = jnp.where(diag_of(b), mine, 0.0)
                    pair_of = [kept, nothing] if b < rows // SUB // 2 else [nothing, kept]
                    blocks.append(jnp.concatenate(pair_of, axis=1))
                tall = jnp.concatenate(blocks, axis=0).astype(BF)
                low[slot] = jnp.dot(
                    tall, stacked(up, which, tiles * LANES), preferred_element_type=F32
                ).astype(BF)
        turned = jnp.dot(
            jnp.concatenate(pieces, axis=0).astype(BF), perm2[...], preferred_element_type=F32
        ).astype(BF)
        for j in range(size):
            slot = c * size + j
            a = turned[j * 2 * tiles : j * 2 * tiles + tiles]
            b = turned[j * 2 * tiles + tiles : (j + 1) * 2 * tiles]
            got2[me, slot] = jnp.where(me == 0, a, b)
            right_out[slot] = jnp.where(me == 0, b, a)

    def third(c):
        for j in range(size):
            slot = c * size + j
            held = exchanged(halves(got2, slot))
            for p in range(positions):
                for high in range(2):
                    order_m[j, pl.ds(positions * high + p, SUB, stride=SUB), :] = held[p][high]
        for j in range(size):
            slot = c * size + j
            delta[slot] = (order_m[j] + low[slot].astype(F32)).astype(BF)

    loads[0].wait()
    loads[1].wait()
    for step in range(1, count):
        lab_copy(step).wait_recv()
    fetch = pltpu.make_async_copy(lab_in, lab_s, lsem.at[0])
    fetch.start()
    fetch.wait()

    def body(i, carry):
        @pl.when(i < chunks)
        def _():
            c = order_of(i, chunks)
            for u in range(SPAN):
                step = c * SPAN + u

                @pl.when(step > 0)
                def _():
                    data_copy(step).wait_recv()

            first(c)
            to_helper(c, mixed, got1, s1, r1).start()
            to_helper(c, rank, got_rank, s2, r2, 2).start()

        @pl.when(i == DEPTH)
        def _():
            loads[2].wait()
            loads[3].wait()

        @pl.when((i >= DEPTH) & (i < chunks + DEPTH))
        def _():
            c = order_of(i - DEPTH, chunks)
            to_helper(c, mixed, got1, s1, r1).wait_recv()
            to_helper(c, rank, got_rank, s2, r2, 2).wait_recv()
            second(c)
            to_helper(c, right_out, got2, s3, r3).start()

        @pl.when(i >= 2 * DEPTH)
        def _():
            c = order_of(i - 2 * DEPTH, chunks)
            to_helper(c, right_out, got2, s3, r3).wait_recv()
            third(c)
            for u in range(SPAN):
                step = c * SPAN + u

                @pl.when(step > 0)
                def _():
                    back_copy(step).start()

                @pl.when(step == 0)
                def _():
                    back[own] = delta[own]

        return carry

    lax.fori_loop(0, chunks + 2 * DEPTH, body, 0)
    for step in range(1, count):
        lab_copy(step).wait_send()
        data_copy(step).wait_send()
    for c in range(chunks):
        to_helper(c, mixed, got1, s1, r1).wait_send()
        to_helper(c, rank, got_rank, s2, r2, 2).wait_send()
        to_helper(c, right_out, got2, s3, r3).wait_send()
    for step in range(1, count):
        back_copy(step).wait()
    load_base.wait()


def finish_kernel(table, base, back, out, total, sem):
    requests, tiles, positions, _ = base.shape
    part = requests // PARTS
    saves = []
    for k in range(PARTS):
        for r in range(k * part, (k + 1) * part):
            added = back[table[1, r]].astype(F32).reshape(tiles, positions, LANES)
            total[r] = (base[r].astype(F32) + added).astype(BF)
        at = pl.ds(k * part, part)
        saves.append(pltpu.make_async_copy(total.at[at], out.at[at], sem.at[k]))
        saves[-1].start()
    for save in saves:
        save.wait()


VM = pl.BlockSpec(memory_space=pltpu.VMEM)
SM = pl.BlockSpec(memory_space=pltpu.SMEM)
HBM = pl.BlockSpec(memory_space=pltpu.HBM)


def local(hidden_in, base_out, adapter_ids, left_blocks, right_blocks, down_rank, up_rank):
    servers = lax.axis_size("server")
    helpers = lax.axis_size("helper")
    requests, positions, width_here = hidden_in.shape
    adapters_here, blocks_here, flat = left_blocks.shape
    rank_width = down_rank.shape[2]
    tiles = width_here // LANES
    rows = positions * tiles
    wide = 2 * LANES
    slots = servers * CAP
    fits = (
        helpers == 2
        and BLOCK == LANES // 2
        and flat == BLOCK * BLOCK
        and blocks_here * helpers == BLOCK
        and 2 * tiles == blocks_here
        and positions == 4
        and rank_width * SUB == LANES
        and width_here == blocks_here * BLOCK
        and servers & (servers - 1) == 0
        and servers % (4 * SPAN) == 0
        and requests % PARTS == 0
        and max(requests, slots) <= LANES
    )
    if not fits:
        return plain(
            hidden_in, base_out, adapter_ids, left_blocks, right_blocks, down_rank, up_rank
        )

    def tiled(array):
        split_rows = array.reshape(requests, positions, tiles, LANES)
        return split_rows.transpose(0, 2, 1, 3)

    dma = pltpu.SemaphoreType.DMA
    by_slot = pltpu.VMEM((slots, rows, LANES), BF)
    chunks = servers // SPAN
    piece = pltpu.VMEM((slots, tiles, wide), BF)
    pieces = pltpu.VMEM((helpers, slots, tiles, wide), BF)
    down = jnp.swapaxes(down_rank, 1, 2)
    labels = (servers, 1, LANES)
    hidden = tiled(hidden_in)
    back, base, table = pl.pallas_call(
        functools.partial(fused_kernel, helpers, servers, adapters_here),
        out_shape=(
            pltpu.VMEM((slots, rows, LANES), BF),
            pltpu.VMEM(hidden.shape, BF),
            pltpu.SMEM((SUB, LANES), I32),
        ),
        in_specs=[HBM] * 7,
        out_specs=(VM, VM, SM),
        scratch_shapes=[
            pltpu.VMEM(left_blocks.shape, BF),
            pltpu.VMEM(right_blocks.shape, BF),
            pltpu.VMEM(down.shape, BF),
            pltpu.VMEM(up_rank.shape, BF),
            pltpu.VMEM((1, requests), I32),
            pltpu.VMEM((requests, tiles, positions, LANES), BF),
            by_slot,
            by_slot,
            pltpu.VMEM((SUB, LANES), I32),
            pltpu.VMEM(labels, I32),
            pltpu.VMEM(labels, I32),
            pltpu.SMEM(labels, I32),
            piece,
            pieces,
            pltpu.VMEM((slots // 2, SUB, LANES), F32),
            pltpu.VMEM((helpers, slots // 2, SUB, LANES), F32),
            piece,
            pieces,
            by_slot,
            by_slot,
            pltpu.VMEM((SPAN * CAP, rows, LANES), F32),
            pltpu.VMEM((wide, wide), BF),
            pltpu.VMEM((wide, wide), BF),
            dma((4,)),
            dma((3,)),
            dma((1,)),
            dma((1,)),
        ]
        + [dma((servers,))] * 4
        + [dma((chunks,))] * 6
        + [dma((servers,))] * 2,
        compiler_params=pltpu.CompilerParams(
            collective_id=0, has_side_effects=True, vmem_limit_bytes=VMEM_LIMIT
        ),
        name="fused",
    )(
        *[
            pltpu.with_memory_space_constraint(x, pltpu.HBM)
            for x in (
                adapter_ids.reshape(1, requests),
                hidden,
                tiled(base_out),
                left_blocks,
                right_blocks,
                down,
                up_rank,
            )
        ]
    )
    out = pl.pallas_call(
        finish_kernel,
        out_shape=jax.ShapeDtypeStruct((requests, tiles, positions, LANES), BF),
        in_specs=[SM, VM, VM],
        out_specs=HBM,
        scratch_shapes=[pltpu.VMEM(hidden.shape, BF), dma((PARTS,))],
        name="finish",
    )(
        pltpu.with_memory_space_constraint(table, pltpu.SMEM),
        pltpu.with_memory_space_constraint(base, pltpu.VMEM),
        pltpu.with_memory_space_constraint(back, pltpu.VMEM),
    )
    return out.transpose(0, 2, 1, 3).reshape(requests, positions, width_here)


def solution(mesh):
    in_specs = (
        P("server", None, "helper"),
        P("server", None, "helper"),
        P("server"),
        P("server", "helper", None),
        P("server", "helper", None),
        P("server", "helper", None),
        P("server", None, "helper"),
    )
    out_specs = P("server", None, "helper")
    return jax.shard_map(local, mesh=mesh, in_specs=in_specs, out_specs=out_specs, check_vma=False)
```

```python
import functools

import jax
import jax.numpy as jnp
from jax import lax
from jax.experimental import pallas as pl
from jax.experimental.pallas import tpu as pltpu
from jax.sharding import PartitionSpec as P

BLOCK = 64
CAP = 2


def plain(hidden_in, base_out, adapter_ids, left_blocks, right_blocks, down_rank, up_rank):
    servers = lax.axis_size("server")
    requests, positions, width_here = hidden_in.shape
    adapters_here = left_blocks.shape[0]
    blocks_here = left_blocks.shape[1]
    block_size = BLOCK
    rank_width = down_rank.shape[2]
    slot_total = servers * CAP
    owners = adapter_ids // adapters_here
    local_id = adapter_ids % adapters_here
    number = jnp.arange(requests)
    earlier = (owners[:, None] == owners[None, :]) & (number[None, :] < number[:, None])
    target = owners * CAP + jnp.sum(earlier.astype(jnp.int32), axis=1)
    placing = (jnp.arange(slot_total)[:, None] == target[None, :]).astype(jnp.bfloat16)
    packed = jnp.dot(
        placing,
        hidden_in.reshape(requests, positions * width_here),
        preferred_element_type=jnp.float32,
    ).astype(jnp.bfloat16)
    labels = jnp.dot(
        placing, (local_id + 1).astype(jnp.bfloat16), preferred_element_type=jnp.float32
    ).astype(jnp.bfloat16)
    arrived, arrived_labels = (
        lax.all_to_all(
            packed.reshape(servers, CAP, positions, width_here),
            "server",
            split_axis=0,
            concat_axis=0,
            tiled=True,
        ),
        lax.all_to_all(
            labels.reshape(servers, CAP), "server", split_axis=0, concat_axis=0, tiled=True
        ),
    )
    row_count = slot_total * positions
    flat_rows = arrived.reshape(row_count, width_here)
    block_rows = arrived.reshape(row_count, blocks_here, block_size)
    slot_labels = arrived_labels.reshape(slot_total, 1).astype(jnp.int32)
    row_labels = jnp.broadcast_to(slot_labels, (slot_total, positions)).reshape(row_count)
    numbers = jnp.arange(adapters_here, dtype=jnp.int32)

    def first_factor(carry, inputs):
        mixed_acc, rank_acc = carry
        left_flat, down_tile, number = inputs
        left_tile = left_flat.reshape(blocks_here, block_size, block_size)
        selected = row_labels == number + 1
        mixed = jnp.einsum(
            "rij,ikj->rik", block_rows, left_tile, preferred_element_type=jnp.float32
        ).astype(jnp.bfloat16)
        mixed_acc = jnp.where(selected[:, None, None], mixed, mixed_acc)
        partial_rank = jnp.dot(flat_rows, down_tile, preferred_element_type=jnp.float32)
        rank_acc = jnp.where(selected[:, None], partial_rank, rank_acc)
        return ((mixed_acc, rank_acc), None)

    start_mixed = jnp.zeros((row_count, blocks_here, block_size), jnp.bfloat16)
    start_rank = jnp.zeros((row_count, rank_width), jnp.float32)
    (mixed_rows, rank_partial), ignored = lax.scan(
        first_factor, (start_mixed, start_rank), (left_blocks, down_rank, numbers)
    )
    turned = lax.all_to_all(mixed_rows, "helper", split_axis=2, concat_axis=1, tiled=True)
    rank_sum = lax.psum(rank_partial, "helper")
    rank_proj = rank_sum.astype(jnp.bfloat16)
    columns_here = turned.shape[2]

    def second_factor(carry, inputs):
        right_acc, low_acc = carry
        right_flat, up_tile, number = inputs
        right_tile = right_flat.reshape(right_flat.shape[0], block_size, block_size)
        selected = row_labels == number + 1
        right_out = jnp.einsum(
            "rik,kmi->rmk", turned, right_tile, preferred_element_type=jnp.float32
        ).astype(jnp.bfloat16)
        right_acc = jnp.where(selected[:, None, None], right_out, right_acc)
        low_out = jnp.dot(rank_proj, up_tile, preferred_element_type=jnp.float32).astype(
            jnp.bfloat16
        )
        low_acc = jnp.where(selected[:, None], low_out, low_acc)
        return ((right_acc, low_acc), None)

    start_right = jnp.zeros((row_count, block_size, columns_here), jnp.bfloat16)
    start_low = jnp.zeros((row_count, width_here), jnp.bfloat16)
    (right_rows, rank_rows), ignored = lax.scan(
        second_factor, (start_right, start_low), (right_blocks, up_rank, numbers)
    )
    monarch_rows = lax.all_to_all(
        right_rows, "helper", split_axis=1, concat_axis=2, tiled=True
    ).reshape(row_count, width_here)
    summed_rows = (monarch_rows.astype(jnp.float32) + rank_rows.astype(jnp.float32)).astype(
        jnp.bfloat16
    )
    back_delta = lax.all_to_all(
        summed_rows.reshape(servers, CAP, positions, width_here),
        "server",
        split_axis=0,
        concat_axis=0,
        tiled=True,
    )
    flat_buffer = back_delta.reshape(slot_total, -1)
    delta = (
        jnp.einsum("sr,sc->rc", placing, flat_buffer, preferred_element_type=jnp.float32)
        .astype(jnp.bfloat16)
        .reshape(requests, positions, width_here)
    )
    total = base_out.astype(jnp.float32) + delta.astype(jnp.float32)
    return total.astype(jnp.bfloat16)


LANES = 128
SUB = 8
SPAN = 2
VMEM_LIMIT = 56 << 20
PARTS = 4
PLAN = (
    ["F0", "F1", "FA", "S0", "FB", "SA", "F2", "S1"]
    + ["FC", "SB", "TA", "F3", "FD", "SC", "TB", "S2"]
    + ["SD", "TC", "T0", "S3", "TD", "T1", "T2", "T3"]
)
MESH = pl.DeviceIdType.MESH
NT = (((1,), (1,)), ((), ()))
BF = jnp.bfloat16
F32 = jnp.float32
I32 = jnp.int32


def iota(shape, dim=1):
    return lax.broadcasted_iota(I32, shape, dim)


def flipped(index, mask):
    other = index
    bit = 1
    while bit <= mask:
        if mask & bit:
            other = other + bit * (1 - 2 * lax.rem(lax.div(index, bit), 2))
        bit *= 2
    return other


def flipped_by(index, mask, count):
    other = index
    bit = 1
    while bit < count:
        has = lax.rem(lax.div(mask, bit), 2)
        other = other + bit * has * (1 - 2 * lax.rem(lax.div(index, bit), 2))
        bit *= 2
    return other


def plan_of(chunks):
    half, quarter = chunks // 2, chunks // 4
    named = dict(zip("0123", range(half)))
    named.update(zip("ABCD", [*range(half + quarter, chunks), *range(half, half + quarter)]))
    return [("FST".index(word[0]), named[word[1]]) for word in PLAN]


def pick(i, listed):
    value = jnp.int32(0)
    for at, c in enumerate(listed):
        if c:
            value = value + jnp.where(i == at, c, 0).astype(I32)
    return value


def expand(x):
    low = iota(x.shape) < LANES // 2
    zero = jnp.zeros_like(x)
    turned = pltpu.roll(x, LANES // 2, 1)
    both = jnp.concatenate(
        [
            jnp.where(low, x, zero),
            jnp.where(low, turned, zero),
            jnp.where(low, zero, turned),
            jnp.where(low, zero, x),
        ],
        axis=0,
    ).astype(BF)
    none = jnp.zeros_like(both)
    return jnp.concatenate(
        [jnp.concatenate([both, none], axis=1), jnp.concatenate([none, both], axis=1)], axis=0
    )


def diagonal(full, number):
    wide = full.shape[1]
    groups = full.shape[0] // (2 * SUB)
    sub = iota((SUB, wide), 0)
    parts = full.reshape(groups, 2, SUB, wide)
    upper = number >= SUB
    sets = []
    for h in range(groups // SUB):
        held = [
            jnp.where(upper, parts[h * SUB + c, 1], parts[h * SUB + c, 0]) for c in range(SUB)
        ]
        for bit in (4, 2, 1):
            here = (sub & bit) > 0
            same = ((number & bit) > 0) == here
            merged = []
            for c in range(bit):
                a, b = held[c], held[c + bit]
                kept = jnp.where(here, b, a)
                moved = jnp.where(here, a, b)
                if 2 * bit == SUB:
                    moved = pltpu.roll(moved, bit, 0)
                else:
                    moved = jnp.where(
                        here, pltpu.roll(moved, bit, 0), pltpu.roll(moved, SUB - bit, 0)
                    )
                merged.append(jnp.where(same, kept, moved))
            held = merged
        sets.append(held[0])
    return sets


def factor(w, which, groups, number, wide):
    chunks = w.shape[2] // wide
    sets = []
    for g, x in enumerate(groups):
        rows = jnp.concatenate(
            [
                w[which, 2 * SUB * g : 2 * SUB * (g + 1), c * wide : (c + 1) * wide]
                for c in range(chunks)
            ],
            axis=0,
        )
        full = lax.dot_general(rows, expand(x), NT, preferred_element_type=F32)
        sets.append(diagonal(full, number))
    return jnp.concatenate([sets[g][h] for h in range(2) for g in range(2)], axis=0)


def exchanged(pieces):
    lane = iota((SUB, LANES))
    first, second = (lane & 16) > 0, (lane & 32) > 0
    result = [[None, None] for _ in range(4)]
    for high in range(2):
        at = slice(high * LANES, (high + 1) * LANES)
        by_g = []
        for h in range(2):
            a, b = pieces[h][0][:, at], pieces[h][1][:, at]
            by_g.append(
                (
                    jnp.where(first, pltpu.roll(b, 16, 1), a),
                    jnp.where(first, b, pltpu.roll(a, LANES - 16, 1)),
                )
            )
        for p0 in range(2):
            a, b = by_g[0][p0], by_g[1][p0]
            result[p0][high] = jnp.where(second, pltpu.roll(b, 32, 1), a)
            result[2 + p0][high] = jnp.where(second, b, pltpu.roll(a, LANES - 32, 1))
    return result


def halves(ref, slot):
    found = []
    for h in range(2):
        both = ref[h, slot].astype(F32)
        found.append((both[:SUB], both[SUB:]))
    return found


def stacked(ref, at, width):
    return jnp.concatenate(
        [ref[at, :, k * LANES : (k + 1) * LANES] for k in range(width // LANES)], axis=0
    )


def fused_kernel(
    helpers, count, adapters,
    ids_any, hid_any, base_any, left_any, right_any, down_any, up_any,
    back, base, table_s,
    left, right, down, up, ids, hid, packed, arrived, table, lab, lab_in,
    mixed, got1, rank, got_rank, right_out, got2, low, delta, order_m, perm1, perm2,
    wsem, isem, tsem, lsem, send, recv, lsend, lrecv, s1, r1, s2, r2, s3, r3, bsend, brecv,
):
    me = lax.axis_index("helper")
    here = lax.axis_index("server")
    other = 1 - me
    slots, rows, _ = packed.shape
    wide = mixed.shape[2]
    positions = 4
    tiles = rows // positions
    cap = slots // count
    chunks = count // SPAN
    size = SPAN * cap
    requests = ids.shape[1]

    barrier = pltpu.get_barrier_semaphore()
    for step in range(1, count):
        pl.semaphore_signal(
            barrier, inc=1, device_id={"server": flipped(here, step)}, device_id_type=MESH
        )
    pl.semaphore_signal(barrier, inc=1, device_id={"helper": other}, device_id_type=MESH)
    load_ids = pltpu.make_async_copy(ids_any, ids, isem.at[0])
    load_ids.start()
    load_hid = pltpu.make_async_copy(hid_any, hid, isem.at[1])
    load_hid.start()
    loads = [
        pltpu.make_async_copy(a, b, wsem.at[i])
        for i, (a, b) in enumerate(
            ((left_any, left), (down_any, down), (right_any, right), (up_any, up))
        )
    ]
    load_base = pltpu.make_async_copy(base_any, base, isem.at[2])

    load_ids.wait()
    for load in loads:
        load.start()
    load_base.start()
    names = ids[...]
    owner = jnp.zeros_like(names)
    for s in range(1, count):
        owner = owner + (names >= s * adapters).astype(I32)
    local = names - owner * adapters
    lane = iota((requests, requests))
    row = iota((requests, requests), 0)

    def column(line):
        return jnp.sum(jnp.where(lane == row, line, 0), axis=1, keepdims=True)

    owner_column = column(owner)
    same_owner = owner_column == owner
    before_line = jnp.sum((same_owner & (row < lane)).astype(I32), axis=0, keepdims=True)
    target_line = (owner ^ here) * cap + before_line
    target_column = column(target_line)
    slot_lane = iota((requests, LANES))
    hit = target_column == slot_lane
    inv_line = jnp.sum(jnp.where(hit, iota((requests, LANES), 0), 0), axis=0, keepdims=True)
    table[...] = jnp.zeros_like(table)
    table[0:1, :] = inv_line
    table[1:2, 0:requests] = target_line
    save = pltpu.make_async_copy(table, table_s, tsem.at[0])
    save.start()
    step_row = iota((count, requests), 0)
    step_line = owner ^ here
    lab_lane = iota((count, LANES))
    labels = jnp.zeros((count, LANES), I32)
    for u in range(cap):
        mine = (step_line == step_row) & (before_line == u)
        found = jnp.sum(jnp.where(mine, local, 0), axis=1, keepdims=True)
        labels = labels + jnp.where(lab_lane == u, found, 0)
    for step in range(count):
        lab[step] = labels[step : step + 1]
    lab_in[0] = labels[0:1]
    pl.semaphore_wait(barrier, count)

    def lab_copy(step):
        return pltpu.make_async_remote_copy(
            src_ref=lab.at[step], dst_ref=lab_in.at[step],
            send_sem=lsend.at[0], recv_sem=lrecv.at[step // SPAN],
            device_id={"server": flipped_by(here, step, count)}, device_id_type=MESH,
        )

    def data_copy(step):
        at = pl.ds(step * cap, cap)
        return pltpu.make_async_remote_copy(
            src_ref=packed.at[at], dst_ref=arrived.at[at],
            send_sem=send.at[0], recv_sem=recv.at[step // SPAN],
            device_id={"server": flipped_by(here, step, count)}, device_id_type=MESH,
        )

    def back_copy(step):
        at = pl.ds(step * cap, cap)
        return pltpu.make_async_remote_copy(
            src_ref=delta.at[at], dst_ref=back.at[at],
            send_sem=bsend.at[0], recv_sem=brecv.at[0],
            device_id={"server": flipped_by(here, step, count)}, device_id_type=MESH,
        )

    def to_helper(c, src, dst, s, r, scale=1):
        at = pl.ds(c * (size // scale), size // scale)
        return pltpu.make_async_remote_copy(
            src_ref=src.at[at], dst_ref=dst.at[me, at],
            send_sem=s.at[0], recv_sem=r.at[c],
            device_id={"helper": other}, device_id_type=MESH,
        )

    for step in range(1, count):
        lab_copy(step).start()
    save.wait()
    load_hid.wait()
    for s in range(slots):
        packed[s] = hid[table_s[0, s]].astype(F32).reshape(rows, LANES).astype(BF)
    issue = []
    for j in range(0, count // 4, SPAN):
        issue += [s + j + u for s in (3 * (count // 4), count // 2) for u in range(SPAN)]
    issue += list(range(1, count // 2))
    for step in issue:
        data_copy(step).start()
    own = pl.ds(0, cap)
    arrived[own] = packed[own]

    src = iota((wide, wide), 0)
    dst = iota((wide, wide))
    q, low32, par = src & 192, src & 31, (src >> 5) & 1
    perm1[...] = (
        (q + (low32 & 3) * 16 + 2 * (low32 >> 2) + par == dst).astype(F32).astype(BF)
    )
    perm2[...] = (
        (q + (low32 >> 3) * 16 + 4 * (low32 & 3) + (low32 & 4) // 2 + par == dst)
        .astype(F32)
        .astype(BF)
    )
    code = iota((SUB, wide))
    low32, par = code & 31, (code >> 5) & 1
    number1 = 2 * (low32 >> 2) + par
    number2 = 4 * (low32 & 3) + (low32 & 4) // 2 + par
    sub = iota((SUB, LANES), 0)
    line = iota((SUB, LANES))
    top = sub < positions
    rank_width = LANES // SUB
    nothing = jnp.zeros((SUB, LANES), F32)

    def diag_of(b):
        return line // rank_width == 2 * (b % (tiles // 4)) + sub // positions

    def names_of(c):
        found = []
        for u in range(SPAN):
            line_of = lab_in[c * SPAN + u]
            found += [line_of[0, j] for j in range(cap)]
        return found

    def first(c):
        named = names_of(c)
        pieces, ranks = [], []
        for j in range(size):
            slot = c * size + j
            which = named[j]
            x = arrived[slot]
            xf = x.astype(F32)
            pieces.append(factor(left, which, [xf[: rows // 2], xf[rows // 2 :]], number1, wide))
            part = lax.dot_general(
                x, stacked(down, which, tiles * LANES), NT, preferred_element_type=F32
            )
            total = None
            for b in range(rows // SUB):
                half = b // (tiles // 4)
                block = part[b * SUB : (b + 1) * SUB, half * LANES : (half + 1) * LANES]
                block = jnp.where(diag_of(b), block, 0.0)
                total = block if total is None else total + block
            ranks.append(total + pltpu.roll(total, positions, 0))
        turned = jnp.dot(
            jnp.concatenate(pieces, axis=0).astype(BF), perm1[...], preferred_element_type=F32
        ).astype(BF)
        for j in range(size):
            slot = c * size + j
            a = turned[j * 2 * tiles : j * 2 * tiles + tiles]
            b = turned[j * 2 * tiles + tiles : (j + 1) * 2 * tiles]
            got1[me, slot] = jnp.where(me == 0, a, b)
            mixed[slot] = jnp.where(me == 0, b, a)
        for k in range(size // 2):
            pair = c * (size // 2) + k
            both = jnp.where(top, ranks[2 * k], ranks[2 * k + 1])
            rank[pair] = both
            got_rank[me, pair] = both

    def second(c):
        named = names_of(c)
        pieces = []
        for k in range(size // 2):
            pair = c * (size // 2) + k
            total = got_rank[0, pair] + got_rank[1, pair]
            for shift in (64, 32, 16):
                total = total + pltpu.roll(total, shift, 1)
            total = total.astype(BF).astype(F32)
            swapped = pltpu.roll(total, positions, 0)
            for u in range(2):
                slot = c * size + 2 * k + u
                which = named[2 * k + u]
                held = exchanged(halves(got1, slot))
                groups = []
                for g in range(2):
                    blocks = []
                    for p in range(positions):
                        a, b = held[p]
                        if g == 0:
                            blocks.append(jnp.where(top, a, pltpu.roll(b, positions, 0)))
                        else:
                            blocks.append(jnp.where(top, pltpu.roll(a, positions, 0), b))
                    groups.append(jnp.concatenate(blocks, axis=0))
                pieces.append(factor(right, which, groups, number2, wide))
                mine = jnp.where(top, total, swapped) if u == 0 else jnp.where(top, swapped, total)
                blocks = []
                for b in range(rows // SUB):
                    kept = jnp.where(diag_of(b), mine, 0.0)
                    pair_of = [kept, nothing] if b < rows // SUB // 2 else [nothing, kept]
                    blocks.append(jnp.concatenate(pair_of, axis=1))
                tall = jnp.concatenate(blocks, axis=0).astype(BF)
                low[slot] = jnp.dot(
                    tall, stacked(up, which, tiles * LANES), preferred_element_type=F32
                ).astype(BF)
        turned = jnp.dot(
            jnp.concatenate(pieces, axis=0).astype(BF), perm2[...], preferred_element_type=F32
        ).astype(BF)
        for j in range(size):
            slot = c * size + j
            a = turned[j * 2 * tiles : j * 2 * tiles + tiles]
            b = turned[j * 2 * tiles + tiles : (j + 1) * 2 * tiles]
            got2[me, slot] = jnp.where(me == 0, a, b)
            right_out[slot] = jnp.where(me == 0, b, a)

    def third(c):
        for j in range(size):
            slot = c * size + j
            held = exchanged(halves(got2, slot))
            for p in range(positions):
                for high in range(2):
                    order_m[j, pl.ds(positions * high + p, SUB, stride=SUB), :] = held[p][high]
        for j in range(size):
            slot = c * size + j
            delta[slot] = (order_m[j] + low[slot].astype(F32)).astype(BF)

    loads[0].wait()
    loads[1].wait()

    def all_of(ref, sem):
        pltpu.make_async_copy(ref, ref, sem).wait()

    def arrive(c):
        @pl.when(c == 0)
        def _():
            all_of(lab_in.at[pl.ds(1, SPAN - 1)], lrecv.at[0])
            all_of(arrived.at[pl.ds(cap, (SPAN - 1) * cap)], recv.at[0])

        @pl.when(c > 0)
        def _():
            all_of(lab_in.at[pl.ds(c * SPAN, SPAN)], lrecv.at[c])
            all_of(arrived.at[pl.ds(c * size, size)], recv.at[c])

    def mid_wait(c):
        to_helper(c, mixed, got1, s1, r1).wait_recv()
        to_helper(c, rank, got_rank, s2, r2, 2).wait_recv()

    def mid_start(c):
        to_helper(c, mixed, got1, s1, r1).start()
        to_helper(c, rank, got_rank, s2, r2, 2).start()

    plan = plan_of(chunks)
    quarter = count // 4
    inner = lax.rem(lax.div(here, quarter), 2) != lax.div(here, 2 * quarter)
    turn = jnp.where(inner, chunks // 4, 0)
    first_second = [stage for stage, _ in plan].index(1)

    def body(i, carry):
        stage, c = pick(i, [s for s, _ in plan]), pick(i, [k for _, k in plan])
        c = c + jnp.where(c >= chunks // 2, turn * (1 - 2 * (c // (chunks // 4) % 2)), 0)

        @pl.when(i == first_second)
        def _():
            loads[2].wait()
            loads[3].wait()

        @pl.when(stage == 0)
        def _():
            arrive(c)
            first(c)
            mid_start(c)

        @pl.when(stage == 1)
        def _():
            mid_wait(c)
            second(c)
            to_helper(c, right_out, got2, s3, r3).start()

        @pl.when(stage == 2)
        def _():
            to_helper(c, right_out, got2, s3, r3).wait_recv()
            third(c)
            for u in range(SPAN):
                step = c * SPAN + u

                @pl.when(step > 0)
                def _():
                    back_copy(step).start()

                @pl.when(step == 0)
                def _():
                    keep = pltpu.make_async_copy(delta.at[own], back.at[own], lsem.at[0])
                    keep.start()
                    keep.wait()

        return carry

    lax.fori_loop(0, len(plan), body, 0)
    rest = pl.ds(1, count - 1)
    others = pl.ds(cap, slots - cap)
    all_of(lab.at[rest], lsend.at[0])
    all_of(packed.at[others], send.at[0])
    all_of(mixed, s1.at[0])
    all_of(rank, s2.at[0])
    all_of(right_out, s3.at[0])
    all_of(delta.at[others], bsend.at[0])
    all_of(back.at[others], brecv.at[0])
    load_base.wait()


def finish_kernel(table, base, back, out, total, sem):
    requests, tiles, positions, _ = base.shape
    part = requests // PARTS
    saves = []
    for k in range(PARTS):
        for r in range(k * part, (k + 1) * part):
            added = back[table[1, r]].astype(F32).reshape(tiles, positions, LANES)
            total[r] = (base[r].astype(F32) + added).astype(BF)
        at = pl.ds(k * part, part)
        saves.append(pltpu.make_async_copy(total.at[at], out.at[at], sem.at[k]))
        saves[-1].start()
    for save in saves:
        save.wait()


VM = pl.BlockSpec(memory_space=pltpu.VMEM)
SM = pl.BlockSpec(memory_space=pltpu.SMEM)
ANY = pl.BlockSpec(memory_space=pl.ANY)
HBM = pl.BlockSpec(memory_space=pltpu.HBM)


def local(hidden_in, base_out, adapter_ids, left_blocks, right_blocks, down_rank, up_rank):
    servers = lax.axis_size("server")
    helpers = lax.axis_size("helper")
    requests, positions, width_here = hidden_in.shape
    adapters_here, blocks_here, flat = left_blocks.shape
    rank_width = down_rank.shape[2]
    tiles = width_here // LANES
    rows = positions * tiles
    wide = 2 * LANES
    slots = servers * CAP
    fits = (
        helpers == 2
        and BLOCK == LANES // 2
        and flat == BLOCK * BLOCK
        and blocks_here * helpers == BLOCK
        and 2 * tiles == blocks_here
        and positions == 4
        and rank_width * SUB == LANES
        and width_here == blocks_here * BLOCK
        and servers & (servers - 1) == 0
        and servers * 3 == len(PLAN) * SPAN
        and requests % PARTS == 0
        and max(requests, slots) <= LANES
    )
    if not fits:
        return plain(
            hidden_in, base_out, adapter_ids, left_blocks, right_blocks, down_rank, up_rank
        )

    def tiled(array):
        split_rows = array.reshape(requests, positions, tiles, LANES)
        return split_rows.transpose(0, 2, 1, 3)

    dma = pltpu.SemaphoreType.DMA
    by_slot = pltpu.VMEM((slots, rows, LANES), BF)
    chunks = servers // SPAN
    piece = pltpu.VMEM((slots, tiles, wide), BF)
    pieces = pltpu.VMEM((helpers, slots, tiles, wide), BF)
    down = jnp.swapaxes(down_rank, 1, 2)
    labels = (servers, 1, LANES)
    hidden = tiled(hidden_in)
    back, base, table = pl.pallas_call(
        functools.partial(fused_kernel, helpers, servers, adapters_here),
        out_shape=(
            pltpu.VMEM((slots, rows, LANES), BF),
            pltpu.VMEM(hidden.shape, BF),
            pltpu.SMEM((SUB, LANES), I32),
        ),
        in_specs=[HBM] * 7,
        out_specs=(ANY, ANY, SM),
        scratch_shapes=[
            pltpu.VMEM(left_blocks.shape, BF),
            pltpu.VMEM(right_blocks.shape, BF),
            pltpu.VMEM(down.shape, BF),
            pltpu.VMEM(up_rank.shape, BF),
            pltpu.VMEM((1, requests), I32),
            pltpu.VMEM((requests, tiles, positions, LANES), BF),
            by_slot,
            by_slot,
            pltpu.VMEM((SUB, LANES), I32),
            pltpu.VMEM(labels, I32),
            pltpu.VMEM(labels, I32),
            piece,
            pieces,
            pltpu.VMEM((slots // 2, SUB, LANES), F32),
            pltpu.VMEM((helpers, slots // 2, SUB, LANES), F32),
            piece,
            pieces,
            by_slot,
            by_slot,
            pltpu.VMEM((SPAN * CAP, rows, LANES), F32),
            pltpu.VMEM((wide, wide), BF),
            pltpu.VMEM((wide, wide), BF),
            dma((4,)),
            dma((3,)),
            dma((1,)),
            dma((1,)),
        ]
        + [dma((1,)), dma((chunks,))] * 5
        + [dma((1,))] * 2,
        compiler_params=pltpu.CompilerParams(
            collective_id=0, has_side_effects=True, vmem_limit_bytes=VMEM_LIMIT
        ),
        name="fused",
    )(
        *[
            pltpu.with_memory_space_constraint(x, pltpu.HBM)
            for x in (
                adapter_ids.reshape(1, requests),
                hidden,
                tiled(base_out),
                left_blocks,
                right_blocks,
                down,
                up_rank,
            )
        ]
    )
    out = pl.pallas_call(
        finish_kernel,
        out_shape=jax.ShapeDtypeStruct((requests, tiles, positions, LANES), BF),
        in_specs=[SM, VM, VM],
        out_specs=HBM,
        scratch_shapes=[pltpu.VMEM(hidden.shape, BF), dma((PARTS,))],
        name="finish",
    )(
        pltpu.with_memory_space_constraint(table, pltpu.SMEM),
        pltpu.with_memory_space_constraint(base, pltpu.VMEM),
        pltpu.with_memory_space_constraint(back, pltpu.VMEM),
    )
    return out.transpose(0, 2, 1, 3).reshape(requests, positions, width_here)


def solution(mesh):
    in_specs = (
        P("server", None, "helper"),
        P("server", None, "helper"),
        P("server"),
        P("server", "helper", None),
        P("server", "helper", None),
        P("server", "helper", None),
        P("server", None, "helper"),
    )
    out_specs = P("server", None, "helper")
    return jax.shard_map(local, mesh=mesh, in_specs=in_specs, out_specs=out_specs, check_vma=False)
```

```python
import functools

import jax
import jax.numpy as jnp
from jax import lax
from jax.experimental import pallas as pl
from jax.experimental.pallas import tpu as pltpu
from jax.sharding import PartitionSpec as P

BLOCK = 64
CAP = 2


def plain(hidden_in, base_out, adapter_ids, left_blocks, right_blocks, down_rank, up_rank):
    servers = lax.axis_size("server")
    requests, positions, width_here = hidden_in.shape
    adapters_here = left_blocks.shape[0]
    blocks_here = left_blocks.shape[1]
    block_size = BLOCK
    rank_width = down_rank.shape[2]
    slot_total = servers * CAP
    owners = adapter_ids // adapters_here
    local_id = adapter_ids % adapters_here
    number = jnp.arange(requests)
    earlier = (owners[:, None] == owners[None, :]) & (number[None, :] < number[:, None])
    target = owners * CAP + jnp.sum(earlier.astype(jnp.int32), axis=1)
    placing = (jnp.arange(slot_total)[:, None] == target[None, :]).astype(jnp.bfloat16)
    packed = jnp.dot(
        placing,
        hidden_in.reshape(requests, positions * width_here),
        preferred_element_type=jnp.float32,
    ).astype(jnp.bfloat16)
    labels = jnp.dot(
        placing, (local_id + 1).astype(jnp.bfloat16), preferred_element_type=jnp.float32
    ).astype(jnp.bfloat16)
    arrived, arrived_labels = (
        lax.all_to_all(
            packed.reshape(servers, CAP, positions, width_here),
            "server",
            split_axis=0,
            concat_axis=0,
            tiled=True,
        ),
        lax.all_to_all(
            labels.reshape(servers, CAP), "server", split_axis=0, concat_axis=0, tiled=True
        ),
    )
    row_count = slot_total * positions
    flat_rows = arrived.reshape(row_count, width_here)
    block_rows = arrived.reshape(row_count, blocks_here, block_size)
    slot_labels = arrived_labels.reshape(slot_total, 1).astype(jnp.int32)
    row_labels = jnp.broadcast_to(slot_labels, (slot_total, positions)).reshape(row_count)
    numbers = jnp.arange(adapters_here, dtype=jnp.int32)

    def first_factor(carry, inputs):
        mixed_acc, rank_acc = carry
        left_flat, down_tile, number = inputs
        left_tile = left_flat.reshape(blocks_here, block_size, block_size)
        selected = row_labels == number + 1
        mixed = jnp.einsum(
            "rij,ikj->rik", block_rows, left_tile, preferred_element_type=jnp.float32
        ).astype(jnp.bfloat16)
        mixed_acc = jnp.where(selected[:, None, None], mixed, mixed_acc)
        partial_rank = jnp.dot(flat_rows, down_tile, preferred_element_type=jnp.float32)
        rank_acc = jnp.where(selected[:, None], partial_rank, rank_acc)
        return ((mixed_acc, rank_acc), None)

    start_mixed = jnp.zeros((row_count, blocks_here, block_size), jnp.bfloat16)
    start_rank = jnp.zeros((row_count, rank_width), jnp.float32)
    (mixed_rows, rank_partial), ignored = lax.scan(
        first_factor, (start_mixed, start_rank), (left_blocks, down_rank, numbers)
    )
    turned = lax.all_to_all(mixed_rows, "helper", split_axis=2, concat_axis=1, tiled=True)
    rank_sum = lax.psum(rank_partial, "helper")
    rank_proj = rank_sum.astype(jnp.bfloat16)
    columns_here = turned.shape[2]

    def second_factor(carry, inputs):
        right_acc, low_acc = carry
        right_flat, up_tile, number = inputs
        right_tile = right_flat.reshape(right_flat.shape[0], block_size, block_size)
        selected = row_labels == number + 1
        right_out = jnp.einsum(
            "rik,kmi->rmk", turned, right_tile, preferred_element_type=jnp.float32
        ).astype(jnp.bfloat16)
        right_acc = jnp.where(selected[:, None, None], right_out, right_acc)
        low_out = jnp.dot(rank_proj, up_tile, preferred_element_type=jnp.float32).astype(
            jnp.bfloat16
        )
        low_acc = jnp.where(selected[:, None], low_out, low_acc)
        return ((right_acc, low_acc), None)

    start_right = jnp.zeros((row_count, block_size, columns_here), jnp.bfloat16)
    start_low = jnp.zeros((row_count, width_here), jnp.bfloat16)
    (right_rows, rank_rows), ignored = lax.scan(
        second_factor, (start_right, start_low), (right_blocks, up_rank, numbers)
    )
    monarch_rows = lax.all_to_all(
        right_rows, "helper", split_axis=1, concat_axis=2, tiled=True
    ).reshape(row_count, width_here)
    summed_rows = (monarch_rows.astype(jnp.float32) + rank_rows.astype(jnp.float32)).astype(
        jnp.bfloat16
    )
    back_delta = lax.all_to_all(
        summed_rows.reshape(servers, CAP, positions, width_here),
        "server",
        split_axis=0,
        concat_axis=0,
        tiled=True,
    )
    flat_buffer = back_delta.reshape(slot_total, -1)
    delta = (
        jnp.einsum("sr,sc->rc", placing, flat_buffer, preferred_element_type=jnp.float32)
        .astype(jnp.bfloat16)
        .reshape(requests, positions, width_here)
    )
    total = base_out.astype(jnp.float32) + delta.astype(jnp.float32)
    return total.astype(jnp.bfloat16)


LANES = 128
SUB = 8
SPAN = 2
VMEM_LIMIT = 56 << 20
PARTS = 4
PLAN = (
    ["F0", "F1", "FA", "S0", "S1", "FB", "SA", "F2"]
    + ["FC", "SB", "TA", "F3", "T0", "S2", "FD", "SC"]
    + ["TB", "T1", "T2", "S3", "SD", "TC", "T3", "TD"]
)
MESH = pl.DeviceIdType.MESH
NT = (((1,), (1,)), ((), ()))
BF = jnp.bfloat16
F32 = jnp.float32
I32 = jnp.int32


def iota(shape, dim=1):
    return lax.broadcasted_iota(I32, shape, dim)


def flipped(index, mask):
    other = index
    bit = 1
    while bit <= mask:
        if mask & bit:
            other = other + bit * (1 - 2 * lax.rem(lax.div(index, bit), 2))
        bit *= 2
    return other


def flipped_by(index, mask, count):
    other = index
    bit = 1
    while bit < count:
        has = lax.rem(lax.div(mask, bit), 2)
        other = other + bit * has * (1 - 2 * lax.rem(lax.div(index, bit), 2))
        bit *= 2
    return other


def plan_of(chunks):
    half, quarter = chunks // 2, chunks // 4
    named = dict(zip("0123", range(half)))
    named.update(zip("ABCD", [*range(half + quarter, chunks), *range(half, half + quarter)]))
    return [("FST".index(word[0]), named[word[1]]) for word in PLAN]


def pick(i, listed):
    value = jnp.int32(0)
    for at, c in enumerate(listed):
        if c:
            value = value + jnp.where(i == at, c, 0).astype(I32)
    return value


def expand(x):
    low = iota(x.shape) < LANES // 2
    zero = jnp.zeros_like(x)
    turned = pltpu.roll(x, LANES // 2, 1)
    both = jnp.concatenate(
        [
            jnp.where(low, x, zero),
            jnp.where(low, turned, zero),
            jnp.where(low, zero, turned),
            jnp.where(low, zero, x),
        ],
        axis=0,
    )
    none = jnp.zeros_like(both)
    return jnp.concatenate(
        [jnp.concatenate([both, none], axis=1), jnp.concatenate([none, both], axis=1)], axis=0
    )


def diagonal(full, number):
    wide = full.shape[1]
    groups = full.shape[0] // (2 * SUB)
    sub = iota((SUB, wide), 0)
    parts = full.reshape(groups, 2, SUB, wide)
    upper = number >= SUB
    sets = []
    for h in range(groups // SUB):
        held = [
            jnp.where(upper, parts[h * SUB + c, 1], parts[h * SUB + c, 0]) for c in range(SUB)
        ]
        for bit in (4, 2, 1):
            here = (sub & bit) > 0
            same = ((number & bit) > 0) == here
            merged = []
            for c in range(bit):
                a, b = held[c], held[c + bit]
                kept = jnp.where(here, b, a)
                moved = jnp.where(here, a, b)
                if 2 * bit == SUB:
                    moved = pltpu.roll(moved, bit, 0)
                else:
                    moved = jnp.where(
                        here, pltpu.roll(moved, bit, 0), pltpu.roll(moved, SUB - bit, 0)
                    )
                merged.append(jnp.where(same, kept, moved))
            held = merged
        sets.append(held[0])
    return sets


def factor(w, which, groups, number, wide):
    chunks = w.shape[2] // wide
    sets = []
    for g, x in enumerate(groups):
        rows = jnp.concatenate(
            [
                w[which, 2 * SUB * g : 2 * SUB * (g + 1), c * wide : (c + 1) * wide]
                for c in range(chunks)
            ],
            axis=0,
        )
        full = lax.dot_general(rows, expand(x), NT, preferred_element_type=F32)
        sets.append(diagonal(full, number))
    return jnp.concatenate([sets[g][h] for h in range(2) for g in range(2)], axis=0)


def exchanged(ref, slot):
    first = (iota((SUB, LANES)) & 16) > 0
    second = (iota((2 * SUB, LANES)) & 32) > 0
    result = [[None, None] for _ in range(4)]
    for high in range(2):
        at = slice(high * LANES, (high + 1) * LANES)
        a, b = ref[0, slot, :, at], ref[1, slot, :, at]
        by_p = (
            jnp.where(second, pltpu.roll(b, 32, 1), a),
            jnp.where(second, b, pltpu.roll(a, LANES - 32, 1)),
        )
        for p1 in range(2):
            both = by_p[p1].astype(F32)
            a, b = both[:SUB], both[SUB:]
            result[2 * p1][high] = jnp.where(first, pltpu.roll(b, 16, 1), a)
            result[2 * p1 + 1][high] = jnp.where(first, b, pltpu.roll(a, LANES - 16, 1))
    return result


def stacked(ref, at, width):
    return jnp.concatenate(
        [ref[at, :, k * LANES : (k + 1) * LANES] for k in range(width // LANES)], axis=0
    )


def fused_kernel(
    helpers, count, adapters,
    ids_any, hid_any, base_any, left_any, right_any, down_any, up_any,
    back, base, table_s,
    left, right, down, up, ids, hid, packed, arrived, table, lab, lab_in,
    mixed, got1, rank, got_rank, right_out, got2, low, delta, order_m, perm1, perm2,
    wsem, isem, tsem, lsem, send, recv, lsend, lrecv, s1, r1, s2, r2, s3, r3, bsend, brecv,
):
    me = lax.axis_index("helper")
    here = lax.axis_index("server")
    other = 1 - me
    slots, rows, _ = packed.shape
    wide = mixed.shape[2]
    positions = 4
    tiles = rows // positions
    cap = slots // count
    chunks = count // SPAN
    size = SPAN * cap
    requests = ids.shape[1]

    barrier = pltpu.get_barrier_semaphore()
    for step in range(1, count):
        pl.semaphore_signal(
            barrier, inc=1, device_id={"server": flipped(here, step)}, device_id_type=MESH
        )
    pl.semaphore_signal(barrier, inc=1, device_id={"helper": other}, device_id_type=MESH)
    load_ids = pltpu.make_async_copy(ids_any, ids, isem.at[0])
    load_ids.start()
    load_hid = pltpu.make_async_copy(hid_any, hid, isem.at[1])
    load_hid.start()
    loads = [
        pltpu.make_async_copy(a, b, wsem.at[i])
        for i, (a, b) in enumerate(
            ((left_any, left), (down_any, down), (right_any, right), (up_any, up))
        )
    ]
    load_base = pltpu.make_async_copy(base_any, base, isem.at[2])

    load_ids.wait()
    loads[0].start()
    loads[1].start()
    names = ids[...]
    owner = jnp.zeros_like(names)
    for s in range(1, count):
        owner = owner + (names >= s * adapters).astype(I32)
    local = names - owner * adapters
    lane = iota((requests, requests))
    row = iota((requests, requests), 0)

    def column(line):
        return jnp.sum(jnp.where(lane == row, line, 0), axis=1, keepdims=True)

    owner_column = column(owner)
    same_owner = owner_column == owner
    before_line = jnp.sum((same_owner & (row < lane)).astype(I32), axis=0, keepdims=True)
    target_line = (owner ^ here) * cap + before_line
    target_column = column(target_line)
    slot_lane = iota((requests, LANES))
    hit = target_column == slot_lane
    inv_line = jnp.sum(jnp.where(hit, iota((requests, LANES), 0), 0), axis=0, keepdims=True)
    table[...] = jnp.zeros_like(table)
    table[0:1, :] = inv_line
    table[1:2, 0:requests] = target_line
    save = pltpu.make_async_copy(table, table_s, tsem.at[0])
    save.start()
    step_row = iota((count, requests), 0)
    step_line = owner ^ here
    lab_lane = iota((count, LANES))
    labels = jnp.zeros((count, LANES), I32)
    for u in range(cap):
        mine = (step_line == step_row) & (before_line == u)
        found = jnp.sum(jnp.where(mine, local, 0), axis=1, keepdims=True)
        labels = labels + jnp.where(lab_lane == u, found, 0)
    for step in range(count):
        lab[step] = labels[step : step + 1]
    lab_in[0] = labels[0:1]
    pl.semaphore_wait(barrier, count)

    def lab_copy(step):
        return pltpu.make_async_remote_copy(
            src_ref=lab.at[step], dst_ref=lab_in.at[step],
            send_sem=lsend.at[0], recv_sem=lrecv.at[step // SPAN],
            device_id={"server": flipped_by(here, step, count)}, device_id_type=MESH,
        )

    def data_copy(step):
        at = pl.ds(step * cap, cap)
        return pltpu.make_async_remote_copy(
            src_ref=packed.at[at], dst_ref=arrived.at[at],
            send_sem=send.at[0], recv_sem=recv.at[step // SPAN],
            device_id={"server": flipped_by(here, step, count)}, device_id_type=MESH,
        )

    def back_copy(step):
        at = pl.ds(step * cap, cap)
        return pltpu.make_async_remote_copy(
            src_ref=delta.at[at], dst_ref=back.at[at],
            send_sem=bsend.at[0], recv_sem=brecv.at[0],
            device_id={"server": flipped_by(here, step, count)}, device_id_type=MESH,
        )

    def to_helper(c, src, dst, s, r, scale=1):
        at = pl.ds(c * (size // scale), size // scale)
        return pltpu.make_async_remote_copy(
            src_ref=src.at[at], dst_ref=dst.at[me, at],
            send_sem=s.at[0], recv_sem=r.at[c],
            device_id={"helper": other}, device_id_type=MESH,
        )

    for step in range(1, count):
        lab_copy(step).start()
    save.wait()
    load_hid.wait()
    for s in range(slots):
        packed[s] = hid[table_s[0, s]].astype(F32).reshape(rows, LANES).astype(BF)
    issue = []
    for j in range(0, count // 4, SPAN):
        issue += [s + j + u for s in (3 * (count // 4), count // 2) for u in range(SPAN)]
    issue += list(range(1, count // 2))
    for step in issue:
        data_copy(step).start()
    own = pl.ds(0, cap)
    arrived[own] = packed[own]

    src = iota((wide, wide), 0)
    dst = iota((wide, wide))
    q, low32, par = src & 192, src & 31, (src >> 5) & 1
    perm1[...] = (
        (q + (low32 & 3) * 16 + 2 * (low32 >> 2) + par == dst).astype(F32).astype(BF)
    )
    perm2[...] = (
        (q + (low32 >> 3) * 16 + 4 * (low32 & 3) + (low32 & 4) // 2 + par == dst)
        .astype(F32)
        .astype(BF)
    )
    code = iota((SUB, wide))
    low32, par = code & 31, (code >> 5) & 1
    number1 = 2 * (low32 >> 2) + par
    number2 = 4 * (low32 & 3) + (low32 & 4) // 2 + par
    sub = iota((SUB, LANES), 0)
    line = iota((SUB, LANES))
    top = sub < positions
    rank_width = LANES // SUB
    nothing = jnp.zeros((SUB, LANES), F32)

    def diag_of(b):
        return line // rank_width == 2 * (b % (tiles // 4)) + sub // positions

    def names_of(c):
        found = []
        for u in range(SPAN):
            line_of = lab_in[c * SPAN + u]
            found += [line_of[0, j] for j in range(cap)]
        return found

    def first(c):
        named = names_of(c)
        pieces, ranks = [], []
        for j in range(size):
            slot = c * size + j
            which = named[j]
            x = arrived[slot]
            pieces.append(factor(left, which, [x[: rows // 2], x[rows // 2 :]], number1, wide))
            part = lax.dot_general(
                x, stacked(down, which, tiles * LANES), NT, preferred_element_type=F32
            )
            total = None
            for b in range(rows // SUB):
                half = b // (tiles // 4)
                block = part[b * SUB : (b + 1) * SUB, half * LANES : (half + 1) * LANES]
                block = jnp.where(diag_of(b), block, 0.0)
                total = block if total is None else total + block
            ranks.append(total + pltpu.roll(total, positions, 0))
        turned = jnp.dot(
            jnp.concatenate(pieces, axis=0).astype(BF), perm1[...], preferred_element_type=F32
        ).astype(BF)
        for j in range(size):
            slot = c * size + j
            a = turned[j * 2 * tiles : j * 2 * tiles + tiles]
            b = turned[j * 2 * tiles + tiles : (j + 1) * 2 * tiles]
            got1[me, slot] = jnp.where(me == 0, a, b)
            mixed[slot] = jnp.where(me == 0, b, a)
        for k in range(size // 2):
            pair = c * (size // 2) + k
            both = jnp.where(top, ranks[2 * k], ranks[2 * k + 1])
            rank[pair] = both
            got_rank[me, pair] = both

    def second(c):
        named = names_of(c)
        pieces = []
        for k in range(size // 2):
            pair = c * (size // 2) + k
            total = got_rank[0, pair] + got_rank[1, pair]
            for shift in (64, 32, 16):
                total = total + pltpu.roll(total, shift, 1)
            total = total.astype(BF).astype(F32)
            swapped = pltpu.roll(total, positions, 0)
            for u in range(2):
                slot = c * size + 2 * k + u
                which = named[2 * k + u]
                held = exchanged(got1, slot)
                groups = []
                for g in range(2):
                    blocks = []
                    for p in range(positions):
                        a, b = held[p]
                        if g == 0:
                            blocks.append(jnp.where(top, a, pltpu.roll(b, positions, 0)))
                        else:
                            blocks.append(jnp.where(top, pltpu.roll(a, positions, 0), b))
                    groups.append(jnp.concatenate(blocks, axis=0).astype(BF))
                pieces.append(factor(right, which, groups, number2, wide))
                mine = jnp.where(top, total, swapped) if u == 0 else jnp.where(top, swapped, total)
                blocks = []
                for b in range(rows // SUB):
                    kept = jnp.where(diag_of(b), mine, 0.0)
                    pair_of = [kept, nothing] if b < rows // SUB // 2 else [nothing, kept]
                    blocks.append(jnp.concatenate(pair_of, axis=1))
                tall = jnp.concatenate(blocks, axis=0).astype(BF)
                low[slot] = jnp.dot(
                    tall, stacked(up, which, tiles * LANES), preferred_element_type=F32
                ).astype(BF)
        turned = jnp.dot(
            jnp.concatenate(pieces, axis=0).astype(BF), perm2[...], preferred_element_type=F32
        ).astype(BF)
        for j in range(size):
            slot = c * size + j
            a = turned[j * 2 * tiles : j * 2 * tiles + tiles]
            b = turned[j * 2 * tiles + tiles : (j + 1) * 2 * tiles]
            got2[me, slot] = jnp.where(me == 0, a, b)
            right_out[slot] = jnp.where(me == 0, b, a)

    def third(c):
        for j in range(size):
            slot = c * size + j
            held = exchanged(got2, slot)
            for p in range(positions):
                for high in range(2):
                    order_m[j, pl.ds(positions * high + p, SUB, stride=SUB), :] = held[p][high]
        for j in range(size):
            slot = c * size + j
            delta[slot] = (order_m[j] + low[slot].astype(F32)).astype(BF)

    loads[0].wait()
    loads[1].wait()
    loads[2].start()
    loads[3].start()
    load_base.start()

    def all_of(ref, sem):
        pltpu.make_async_copy(ref, ref, sem).wait()

    def arrive(c):
        @pl.when(c == 0)
        def _():
            all_of(lab_in.at[pl.ds(1, SPAN - 1)], lrecv.at[0])
            all_of(arrived.at[pl.ds(cap, (SPAN - 1) * cap)], recv.at[0])

        @pl.when(c > 0)
        def _():
            all_of(lab_in.at[pl.ds(c * SPAN, SPAN)], lrecv.at[c])
            all_of(arrived.at[pl.ds(c * size, size)], recv.at[c])

    def mid_wait(c):
        to_helper(c, mixed, got1, s1, r1).wait_recv()
        to_helper(c, rank, got_rank, s2, r2, 2).wait_recv()

    def mid_start(c):
        to_helper(c, mixed, got1, s1, r1).start()
        to_helper(c, rank, got_rank, s2, r2, 2).start()

    plan = plan_of(chunks)
    quarter = count // 4
    inner = lax.rem(lax.div(here, quarter), 2) != lax.div(here, 2 * quarter)
    turn = jnp.where(inner, chunks // 4, 0)
    first_second = [stage for stage, _ in plan].index(1)

    def turned_of(c):
        return c + jnp.where(c >= chunks // 2, turn * (1 - 2 * (c // (chunks // 4) % 2)), 0)

    def body(i, carry):
        stage, c = (pick(i, [entry[k] for entry in plan]) for k in range(2))
        c = turned_of(c)

        @pl.when(i == first_second)
        def _():
            loads[2].wait()
            loads[3].wait()

        @pl.when(stage == 0)
        def _():
            arrive(c)
            first(c)
            mid_start(c)

        @pl.when(stage == 1)
        def _():
            mid_wait(c)
            second(c)
            to_helper(c, right_out, got2, s3, r3).start()

        @pl.when(stage == 2)
        def _():
            to_helper(c, right_out, got2, s3, r3).wait_recv()
            third(c)
            for u in range(SPAN):
                step = c * SPAN + u

                @pl.when(step > 0)
                def _():
                    back_copy(step).start()

                @pl.when(step == 0)
                def _():
                    keep = pltpu.make_async_copy(delta.at[own], back.at[own], lsem.at[0])
                    keep.start()
                    keep.wait()

        return carry

    lax.fori_loop(0, len(plan), body, 0)
    rest = pl.ds(1, count - 1)
    others = pl.ds(cap, slots - cap)
    all_of(lab.at[rest], lsend.at[0])
    all_of(packed.at[others], send.at[0])
    all_of(mixed, s1.at[0])
    all_of(rank, s2.at[0])
    all_of(right_out, s3.at[0])
    all_of(delta.at[others], bsend.at[0])
    all_of(back.at[others], brecv.at[0])
    load_base.wait()


def finish_kernel(table, base, back, out, total, sem):
    requests, tiles, positions, _ = base.shape
    part = requests // PARTS
    saves = []
    for k in range(PARTS):
        for r in range(k * part, (k + 1) * part):
            added = back[table[1, r]].astype(F32).reshape(tiles, positions, LANES)
            total[r] = (base[r].astype(F32) + added).astype(BF)
        at = pl.ds(k * part, part)
        saves.append(pltpu.make_async_copy(total.at[at], out.at[at], sem.at[k]))
        saves[-1].start()
    for save in saves:
        save.wait()


VM = pl.BlockSpec(memory_space=pltpu.VMEM)
SM = pl.BlockSpec(memory_space=pltpu.SMEM)
ANY = pl.BlockSpec(memory_space=pl.ANY)
HBM = pl.BlockSpec(memory_space=pltpu.HBM)


def local(hidden_in, base_out, adapter_ids, left_blocks, right_blocks, down_rank, up_rank):
    servers = lax.axis_size("server")
    helpers = lax.axis_size("helper")
    requests, positions, width_here = hidden_in.shape
    adapters_here, blocks_here, flat = left_blocks.shape
    rank_width = down_rank.shape[2]
    tiles = width_here // LANES
    rows = positions * tiles
    wide = 2 * LANES
    slots = servers * CAP
    fits = (
        helpers == 2
        and BLOCK == LANES // 2
        and flat == BLOCK * BLOCK
        and blocks_here * helpers == BLOCK
        and 2 * tiles == blocks_here
        and positions == 4
        and rank_width * SUB == LANES
        and width_here == blocks_here * BLOCK
        and servers & (servers - 1) == 0
        and servers == 8 * SPAN
        and requests % PARTS == 0
        and max(requests, slots) <= LANES
    )
    if not fits:
        return plain(
            hidden_in, base_out, adapter_ids, left_blocks, right_blocks, down_rank, up_rank
        )

    def tiled(array):
        split_rows = array.reshape(requests, positions, tiles, LANES)
        return split_rows.transpose(0, 2, 1, 3)

    dma = pltpu.SemaphoreType.DMA
    by_slot = pltpu.VMEM((slots, rows, LANES), BF)
    chunks = servers // SPAN
    piece = pltpu.VMEM((slots, tiles, wide), BF)
    pieces = pltpu.VMEM((helpers, slots, tiles, wide), BF)
    down = jnp.swapaxes(down_rank, 1, 2)
    labels = (servers, 1, LANES)
    hidden = tiled(hidden_in)
    back, base, table = pl.pallas_call(
        functools.partial(fused_kernel, helpers, servers, adapters_here),
        out_shape=(
            pltpu.VMEM((slots, rows, LANES), BF),
            pltpu.VMEM(hidden.shape, BF),
            pltpu.SMEM((SUB, LANES), I32),
        ),
        in_specs=[HBM] * 7,
        out_specs=(ANY, ANY, SM),
        scratch_shapes=[
            pltpu.VMEM(left_blocks.shape, BF),
            pltpu.VMEM(right_blocks.shape, BF),
            pltpu.VMEM(down.shape, BF),
            pltpu.VMEM(up_rank.shape, BF),
            pltpu.VMEM((1, requests), I32),
            pltpu.VMEM((requests, tiles, positions, LANES), BF),
            by_slot,
            by_slot,
            pltpu.VMEM((SUB, LANES), I32),
            pltpu.VMEM(labels, I32),
            pltpu.VMEM(labels, I32),
            piece,
            pieces,
            pltpu.VMEM((slots // 2, SUB, LANES), F32),
            pltpu.VMEM((helpers, slots // 2, SUB, LANES), F32),
            piece,
            pieces,
            by_slot,
            by_slot,
            pltpu.VMEM((SPAN * CAP, rows, LANES), F32),
            pltpu.VMEM((wide, wide), BF),
            pltpu.VMEM((wide, wide), BF),
            dma((4,)),
            dma((3,)),
            dma((1,)),
            dma((1,)),
        ]
        + [dma((1,)), dma((chunks,))] * 5
        + [dma((1,))] * 2,
        compiler_params=pltpu.CompilerParams(
            collective_id=0, has_side_effects=True, vmem_limit_bytes=VMEM_LIMIT
        ),
        name="fused",
    )(
        *[
            pltpu.with_memory_space_constraint(x, pltpu.HBM)
            for x in (
                adapter_ids.reshape(1, requests),
                hidden,
                tiled(base_out),
                left_blocks,
                right_blocks,
                down,
                up_rank,
            )
        ]
    )
    out = pl.pallas_call(
        finish_kernel,
        out_shape=jax.ShapeDtypeStruct((requests, tiles, positions, LANES), BF),
        in_specs=[SM, VM, VM],
        out_specs=HBM,
        scratch_shapes=[pltpu.VMEM(hidden.shape, BF), dma((PARTS,))],
        name="finish",
    )(
        pltpu.with_memory_space_constraint(table, pltpu.SMEM),
        pltpu.with_memory_space_constraint(base, pltpu.VMEM),
        pltpu.with_memory_space_constraint(back, pltpu.VMEM),
    )
    return out.transpose(0, 2, 1, 3).reshape(requests, positions, width_here)


def solution(mesh):
    in_specs = (
        P("server", None, "helper"),
        P("server", None, "helper"),
        P("server"),
        P("server", "helper", None),
        P("server", "helper", None),
        P("server", "helper", None),
        P("server", None, "helper"),
    )
    out_specs = P("server", None, "helper")
    return jax.shard_map(local, mesh=mesh, in_specs=in_specs, out_specs=out_specs, check_vma=False)
```

```python
import functools

import jax
import jax.numpy as jnp
from jax import lax
from jax.experimental import pallas as pl
from jax.experimental.pallas import tpu as pltpu
from jax.sharding import PartitionSpec as P

BLOCK = 64
CAP = 2


def plain(hidden_in, base_out, adapter_ids, left_blocks, right_blocks, down_rank, up_rank):
    servers = lax.axis_size("server")
    requests, positions, width_here = hidden_in.shape
    adapters_here = left_blocks.shape[0]
    blocks_here = left_blocks.shape[1]
    block_size = BLOCK
    rank_width = down_rank.shape[2]
    slot_total = servers * CAP
    owners = adapter_ids // adapters_here
    local_id = adapter_ids % adapters_here
    number = jnp.arange(requests)
    earlier = (owners[:, None] == owners[None, :]) & (number[None, :] < number[:, None])
    target = owners * CAP + jnp.sum(earlier.astype(jnp.int32), axis=1)
    placing = (jnp.arange(slot_total)[:, None] == target[None, :]).astype(jnp.bfloat16)
    packed = jnp.dot(
        placing,
        hidden_in.reshape(requests, positions * width_here),
        preferred_element_type=jnp.float32,
    ).astype(jnp.bfloat16)
    labels = jnp.dot(
        placing, (local_id + 1).astype(jnp.bfloat16), preferred_element_type=jnp.float32
    ).astype(jnp.bfloat16)
    arrived, arrived_labels = (
        lax.all_to_all(
            packed.reshape(servers, CAP, positions, width_here),
            "server",
            split_axis=0,
            concat_axis=0,
            tiled=True,
        ),
        lax.all_to_all(
            labels.reshape(servers, CAP), "server", split_axis=0, concat_axis=0, tiled=True
        ),
    )
    row_count = slot_total * positions
    flat_rows = arrived.reshape(row_count, width_here)
    block_rows = arrived.reshape(row_count, blocks_here, block_size)
    slot_labels = arrived_labels.reshape(slot_total, 1).astype(jnp.int32)
    row_labels = jnp.broadcast_to(slot_labels, (slot_total, positions)).reshape(row_count)
    numbers = jnp.arange(adapters_here, dtype=jnp.int32)

    def first_factor(carry, inputs):
        mixed_acc, rank_acc = carry
        left_flat, down_tile, number = inputs
        left_tile = left_flat.reshape(blocks_here, block_size, block_size)
        selected = row_labels == number + 1
        mixed = jnp.einsum(
            "rij,ikj->rik", block_rows, left_tile, preferred_element_type=jnp.float32
        ).astype(jnp.bfloat16)
        mixed_acc = jnp.where(selected[:, None, None], mixed, mixed_acc)
        partial_rank = jnp.dot(flat_rows, down_tile, preferred_element_type=jnp.float32)
        rank_acc = jnp.where(selected[:, None], partial_rank, rank_acc)
        return ((mixed_acc, rank_acc), None)

    start_mixed = jnp.zeros((row_count, blocks_here, block_size), jnp.bfloat16)
    start_rank = jnp.zeros((row_count, rank_width), jnp.float32)
    (mixed_rows, rank_partial), ignored = lax.scan(
        first_factor, (start_mixed, start_rank), (left_blocks, down_rank, numbers)
    )
    turned = lax.all_to_all(mixed_rows, "helper", split_axis=2, concat_axis=1, tiled=True)
    rank_sum = lax.psum(rank_partial, "helper")
    rank_proj = rank_sum.astype(jnp.bfloat16)
    columns_here = turned.shape[2]

    def second_factor(carry, inputs):
        right_acc, low_acc = carry
        right_flat, up_tile, number = inputs
        right_tile = right_flat.reshape(right_flat.shape[0], block_size, block_size)
        selected = row_labels == number + 1
        right_out = jnp.einsum(
            "rik,kmi->rmk", turned, right_tile, preferred_element_type=jnp.float32
        ).astype(jnp.bfloat16)
        right_acc = jnp.where(selected[:, None, None], right_out, right_acc)
        low_out = jnp.dot(rank_proj, up_tile, preferred_element_type=jnp.float32).astype(
            jnp.bfloat16
        )
        low_acc = jnp.where(selected[:, None], low_out, low_acc)
        return ((right_acc, low_acc), None)

    start_right = jnp.zeros((row_count, block_size, columns_here), jnp.bfloat16)
    start_low = jnp.zeros((row_count, width_here), jnp.bfloat16)
    (right_rows, rank_rows), ignored = lax.scan(
        second_factor, (start_right, start_low), (right_blocks, up_rank, numbers)
    )
    monarch_rows = lax.all_to_all(
        right_rows, "helper", split_axis=1, concat_axis=2, tiled=True
    ).reshape(row_count, width_here)
    summed_rows = (monarch_rows.astype(jnp.float32) + rank_rows.astype(jnp.float32)).astype(
        jnp.bfloat16
    )
    back_delta = lax.all_to_all(
        summed_rows.reshape(servers, CAP, positions, width_here),
        "server",
        split_axis=0,
        concat_axis=0,
        tiled=True,
    )
    flat_buffer = back_delta.reshape(slot_total, -1)
    delta = (
        jnp.einsum("sr,sc->rc", placing, flat_buffer, preferred_element_type=jnp.float32)
        .astype(jnp.bfloat16)
        .reshape(requests, positions, width_here)
    )
    total = base_out.astype(jnp.float32) + delta.astype(jnp.float32)
    return total.astype(jnp.bfloat16)


LANES = 128
SUB = 8
SPAN = 2
VMEM_LIMIT = 56 << 20
PARTS = 4
PLAN = (
    ["F0", "F1", "FA", "S0", "S1", "FB", "SA", "F2"]
    + ["FC", "SB", "TA", "F3", "T0", "S2", "FD", "SC"]
    + ["TB", "T1", "T2", "S3", "SD", "TC", "T3", "TD"]
)
MESH = pl.DeviceIdType.MESH
NT = (((1,), (1,)), ((), ()))
BF = jnp.bfloat16
F32 = jnp.float32
I32 = jnp.int32


def iota(shape, dim=1):
    return lax.broadcasted_iota(I32, shape, dim)


def flipped(index, mask):
    other = index
    bit = 1
    while bit <= mask:
        if mask & bit:
            other = other + bit * (1 - 2 * lax.rem(lax.div(index, bit), 2))
        bit *= 2
    return other


def flipped_by(index, mask, count):
    other = index
    bit = 1
    while bit < count:
        has = lax.rem(lax.div(mask, bit), 2)
        other = other + bit * has * (1 - 2 * lax.rem(lax.div(index, bit), 2))
        bit *= 2
    return other


def plan_of(chunks):
    half, quarter = chunks // 2, chunks // 4
    named = dict(zip("0123", range(half)))
    named.update(zip("ABCD", [*range(half + quarter, chunks), *range(half, half + quarter)]))
    return [("FST".index(word[0]), named[word[1]]) for word in PLAN]


def pick(i, listed):
    value = jnp.asarray(listed[0], I32)
    for at, c in enumerate(listed[1:]):
        value = jnp.where(i == at + 1, jnp.asarray(c, I32), value)
    return value


def expand(x):
    low = iota(x.shape) < LANES // 2
    zero = jnp.zeros_like(x)
    turned = pltpu.roll(x, LANES // 2, 1)
    both = jnp.concatenate(
        [
            jnp.where(low, x, zero),
            jnp.where(low, turned, zero),
            jnp.where(low, zero, turned),
            jnp.where(low, zero, x),
        ],
        axis=0,
    )
    none = jnp.zeros_like(both)
    return jnp.concatenate(
        [jnp.concatenate([both, none], axis=1), jnp.concatenate([none, both], axis=1)], axis=0
    )


def diagonal(full, number):
    wide = full.shape[1]
    groups = full.shape[0] // (2 * SUB)
    sub = iota((SUB, wide), 0)
    parts = full.reshape(groups, 2, SUB, wide)
    upper = number >= SUB
    sets = []
    for h in range(groups // SUB):
        held = [
            jnp.where(upper, parts[h * SUB + c, 1], parts[h * SUB + c, 0]) for c in range(SUB)
        ]
        for bit in (4, 2, 1):
            here = (sub & bit) > 0
            same = ((number & bit) > 0) == here
            merged = []
            for c in range(bit):
                a, b = held[c], held[c + bit]
                kept = jnp.where(here, b, a)
                moved = jnp.where(here, a, b)
                if 2 * bit == SUB:
                    moved = pltpu.roll(moved, bit, 0)
                else:
                    moved = jnp.where(
                        here, pltpu.roll(moved, bit, 0), pltpu.roll(moved, SUB - bit, 0)
                    )
                merged.append(jnp.where(same, kept, moved))
            held = merged
        sets.append(held[0])
    return sets


def factor(w, which, groups, number, wide):
    chunks = w.shape[2] // wide
    sets = []
    for g, x in enumerate(groups):
        rows = jnp.concatenate(
            [
                w[which, 2 * SUB * g : 2 * SUB * (g + 1), c * wide : (c + 1) * wide]
                for c in range(chunks)
            ],
            axis=0,
        )
        full = lax.dot_general(rows, expand(x), NT, preferred_element_type=F32)
        sets.append(diagonal(full, number))
    return jnp.concatenate([sets[g][h] for h in range(2) for g in range(2)], axis=0)


def exchanged(ref, slot):
    first = (iota((SUB, LANES)) & 16) > 0
    second = (iota((2 * SUB, LANES)) & 32) > 0
    result = [[None, None] for _ in range(4)]
    for high in range(2):
        at = slice(high * LANES, (high + 1) * LANES)
        a, b = ref[0, slot, :, at], ref[1, slot, :, at]
        by_p = (
            jnp.where(second, pltpu.roll(b, 32, 1), a),
            jnp.where(second, b, pltpu.roll(a, LANES - 32, 1)),
        )
        for p1 in range(2):
            both = by_p[p1].astype(F32)
            a, b = both[:SUB], both[SUB:]
            result[2 * p1][high] = jnp.where(first, pltpu.roll(b, 16, 1), a)
            result[2 * p1 + 1][high] = jnp.where(first, b, pltpu.roll(a, LANES - 16, 1))
    return result


def stacked(ref, at, width):
    return jnp.concatenate(
        [ref[at, :, k * LANES : (k + 1) * LANES] for k in range(width // LANES)], axis=0
    )


def fused_kernel(
    helpers, count, adapters,
    ids_any, hid_any, base_any, left_any, right_any, down_any, up_any,
    back, base, table_s,
    left, right, down, up, ids, hid, packed, arrived, table, lab, lab_in,
    mixed, got1, rank, got_rank, right_out, got2, low, delta, order_m, perm1, perm2,
    wsem, isem, tsem, lsem, send, recv, lsend, lrecv, s1, r1, s2, r2, s3, r3, bsend, brecv,
):
    me = lax.axis_index("helper")
    here = lax.axis_index("server")
    other = 1 - me
    slots, rows, _ = packed.shape
    wide = mixed.shape[2]
    positions = 4
    tiles = rows // positions
    cap = slots // count
    chunks = count // SPAN
    size = SPAN * cap
    requests = ids.shape[1]

    barrier = pltpu.get_barrier_semaphore()
    for step in range(1, count):
        pl.semaphore_signal(
            barrier, inc=1, device_id={"server": flipped(here, step)}, device_id_type=MESH
        )
    pl.semaphore_signal(barrier, inc=1, device_id={"helper": other}, device_id_type=MESH)
    load_ids = pltpu.make_async_copy(ids_any, ids, isem.at[0])
    load_ids.start()
    load_hid = pltpu.make_async_copy(hid_any, hid, isem.at[1])
    load_hid.start()
    loads = [
        pltpu.make_async_copy(a, b, wsem.at[i])
        for i, (a, b) in enumerate(
            ((left_any, left), (down_any, down), (right_any, right), (up_any, up))
        )
    ]
    load_base = pltpu.make_async_copy(base_any, base, isem.at[2])

    load_ids.wait()
    loads[0].start()
    loads[1].start()
    names = ids[...]
    owner = jnp.zeros_like(names)
    for s in range(1, count):
        owner = owner + (names >= s * adapters).astype(I32)
    local = names - owner * adapters
    lane = iota((requests, requests))
    row = iota((requests, requests), 0)

    def column(line):
        return jnp.sum(jnp.where(lane == row, line, 0), axis=1, keepdims=True)

    owner_column = column(owner)
    same_owner = owner_column == owner
    before_line = jnp.sum((same_owner & (row < lane)).astype(I32), axis=0, keepdims=True)
    target_line = (owner ^ here) * cap + before_line
    target_column = column(target_line)
    slot_lane = iota((requests, LANES))
    hit = target_column == slot_lane
    inv_line = jnp.sum(jnp.where(hit, iota((requests, LANES), 0), 0), axis=0, keepdims=True)
    table[...] = jnp.zeros_like(table)
    table[0:1, :] = inv_line
    table[1:2, 0:requests] = target_line
    save = pltpu.make_async_copy(table, table_s, tsem.at[0])
    save.start()
    step_row = iota((count, requests), 0)
    step_line = owner ^ here
    lab_lane = iota((count, LANES))
    labels = jnp.zeros((count, LANES), I32)
    for u in range(cap):
        mine = (step_line == step_row) & (before_line == u)
        found = jnp.sum(jnp.where(mine, local, 0), axis=1, keepdims=True)
        labels = labels + jnp.where(lab_lane == u, found, 0)
    for step in range(count):
        lab[step] = labels[step : step + 1]
    lab_in[0] = labels[0:1]
    pl.semaphore_wait(barrier, count)

    def lab_copy(step):
        return pltpu.make_async_remote_copy(
            src_ref=lab.at[step], dst_ref=lab_in.at[step],
            send_sem=lsend.at[0], recv_sem=lrecv.at[step // SPAN],
            device_id={"server": flipped_by(here, step, count)}, device_id_type=MESH,
        )

    def data_copy(step):
        at = pl.ds(step * cap, cap)
        return pltpu.make_async_remote_copy(
            src_ref=packed.at[at], dst_ref=arrived.at[at],
            send_sem=send.at[0], recv_sem=recv.at[step // SPAN],
            device_id={"server": flipped_by(here, step, count)}, device_id_type=MESH,
        )

    def back_copy(step):
        at = pl.ds(step * cap, cap)
        return pltpu.make_async_remote_copy(
            src_ref=delta.at[at], dst_ref=back.at[at],
            send_sem=bsend.at[0], recv_sem=brecv.at[0],
            device_id={"server": flipped_by(here, step, count)}, device_id_type=MESH,
        )

    def to_helper(c, src, dst, s, r, scale=1):
        at = pl.ds(c * (size // scale), size // scale)
        return pltpu.make_async_remote_copy(
            src_ref=src.at[at], dst_ref=dst.at[me, at],
            send_sem=s.at[0], recv_sem=r.at[c],
            device_id={"helper": other}, device_id_type=MESH,
        )

    for step in range(1, count):
        lab_copy(step).start()
    save.wait()
    load_hid.wait()
    for s in range(slots):
        packed[s] = hid[table_s[0, s]].astype(F32).reshape(rows, LANES).astype(BF)
    issue = []
    for j in range(0, count // 4, SPAN):
        issue += [s + j + u for s in (3 * (count // 4), count // 2) for u in range(SPAN)]
    issue += list(range(1, count // 2))
    for step in issue:
        data_copy(step).start()
    own = pl.ds(0, cap)
    arrived[own] = packed[own]

    src = iota((wide, wide), 0)
    dst = iota((wide, wide))
    q, low32, par = src & 192, src & 31, (src >> 5) & 1
    perm1[...] = (
        (q + (low32 & 3) * 16 + 2 * (low32 >> 2) + par == dst).astype(F32).astype(BF)
    )
    perm2[...] = (
        (q + (low32 >> 3) * 16 + 4 * (low32 & 3) + (low32 & 4) // 2 + par == dst)
        .astype(F32)
        .astype(BF)
    )
    code = iota((SUB, wide))
    low32, par = code & 31, (code >> 5) & 1
    number1 = 2 * (low32 >> 2) + par
    number2 = 4 * (low32 & 3) + (low32 & 4) // 2 + par
    sub = iota((SUB, LANES), 0)
    line = iota((SUB, LANES))
    top = sub < positions
    rank_width = LANES // SUB
    nothing = jnp.zeros((SUB, LANES), F32)

    def diag_of(b):
        return line // rank_width == 2 * (b % (tiles // 4)) + sub // positions

    def names_of(c):
        found = []
        for u in range(SPAN):
            line_of = lab_in[c * SPAN + u]
            found += [line_of[0, j] for j in range(cap)]
        return found

    def first(c):
        named = names_of(c)
        pieces, ranks = [], []
        for j in range(size):
            slot = c * size + j
            which = named[j]
            x = arrived[slot]
            pieces.append(factor(left, which, [x[: rows // 2], x[rows // 2 :]], number1, wide))
            part = lax.dot_general(
                x, stacked(down, which, tiles * LANES), NT, preferred_element_type=F32
            )
            total = None
            for b in range(rows // SUB):
                half = b // (tiles // 4)
                block = part[b * SUB : (b + 1) * SUB, half * LANES : (half + 1) * LANES]
                block = jnp.where(diag_of(b), block, 0.0)
                total = block if total is None else total + block
            ranks.append(total + pltpu.roll(total, positions, 0))
        turned = jnp.dot(
            jnp.concatenate(pieces, axis=0).astype(BF), perm1[...], preferred_element_type=F32
        ).astype(BF)
        for j in range(size):
            slot = c * size + j
            a = turned[j * 2 * tiles : j * 2 * tiles + tiles]
            b = turned[j * 2 * tiles + tiles : (j + 1) * 2 * tiles]
            got1[me, slot] = jnp.where(me == 0, a, b)
            mixed[slot] = jnp.where(me == 0, b, a)
        for k in range(size // 2):
            pair = c * (size // 2) + k
            both = jnp.where(top, ranks[2 * k], ranks[2 * k + 1])
            rank[pair] = both
            got_rank[me, pair] = both

    def second(c):
        named = names_of(c)
        pieces = []
        for k in range(size // 2):
            pair = c * (size // 2) + k
            total = got_rank[0, pair] + got_rank[1, pair]
            for shift in (64, 32, 16):
                total = total + pltpu.roll(total, shift, 1)
            total = total.astype(BF).astype(F32)
            swapped = pltpu.roll(total, positions, 0)
            for u in range(2):
                slot = c * size + 2 * k + u
                which = named[2 * k + u]
                held = exchanged(got1, slot)
                groups = []
                for g in range(2):
                    blocks = []
                    for p in range(positions):
                        a, b = held[p]
                        if g == 0:
                            blocks.append(jnp.where(top, a, pltpu.roll(b, positions, 0)))
                        else:
                            blocks.append(jnp.where(top, pltpu.roll(a, positions, 0), b))
                    groups.append(jnp.concatenate(blocks, axis=0).astype(BF))
                pieces.append(factor(right, which, groups, number2, wide))
                mine = jnp.where(top, total, swapped) if u == 0 else jnp.where(top, swapped, total)
                blocks = []
                for b in range(rows // SUB):
                    kept = jnp.where(diag_of(b), mine, 0.0)
                    pair_of = [kept, nothing] if b < rows // SUB // 2 else [nothing, kept]
                    blocks.append(jnp.concatenate(pair_of, axis=1))
                tall = jnp.concatenate(blocks, axis=0).astype(BF)
                low[slot] = jnp.dot(
                    tall, stacked(up, which, tiles * LANES), preferred_element_type=F32
                ).astype(BF)
        turned = jnp.dot(
            jnp.concatenate(pieces, axis=0).astype(BF), perm2[...], preferred_element_type=F32
        ).astype(BF)
        for j in range(size):
            slot = c * size + j
            a = turned[j * 2 * tiles : j * 2 * tiles + tiles]
            b = turned[j * 2 * tiles + tiles : (j + 1) * 2 * tiles]
            got2[me, slot] = jnp.where(me == 0, a, b)
            right_out[slot] = jnp.where(me == 0, b, a)

    def third(c):
        for j in range(size):
            slot = c * size + j
            held = exchanged(got2, slot)
            for p in range(positions):
                for high in range(2):
                    order_m[j, pl.ds(positions * high + p, SUB, stride=SUB), :] = held[p][high]
        for j in range(size):
            slot = c * size + j
            delta[slot] = (order_m[j] + low[slot].astype(F32)).astype(BF)

    loads[0].wait()
    loads[1].wait()
    loads[2].start()
    loads[3].start()
    load_base.start()

    def all_of(ref, sem):
        pltpu.make_async_copy(ref, ref, sem).wait()

    def arrive(c):
        @pl.when(c == 0)
        def _():
            all_of(lab_in.at[pl.ds(1, SPAN - 1)], lrecv.at[0])
            all_of(arrived.at[pl.ds(cap, (SPAN - 1) * cap)], recv.at[0])

        @pl.when(c > 0)
        def _():
            all_of(lab_in.at[pl.ds(c * SPAN, SPAN)], lrecv.at[c])
            all_of(arrived.at[pl.ds(c * size, size)], recv.at[c])

    def mid_wait(c):
        to_helper(c, mixed, got1, s1, r1).wait_recv()
        to_helper(c, rank, got_rank, s2, r2, 2).wait_recv()

    def mid_start(c):
        to_helper(c, mixed, got1, s1, r1).start()
        to_helper(c, rank, got_rank, s2, r2, 2).start()

    plan = plan_of(chunks)
    quarter = count // 4
    inner = lax.rem(lax.div(here, quarter), 2) != lax.div(here, 2 * quarter)
    turn = jnp.where(inner, chunks // 4, 0)
    first_second = [stage for stage, _ in plan].index(1)

    def turned_of(c):
        return c + turn * (1 - 2 * (c // (chunks // 4) % 2)) if c >= chunks // 2 else c

    def body(i, carry):
        code = pick(i, [stage * chunks + c for stage, c in plan])
        stage, c = code // chunks, code % chunks
        c = c + jnp.where(c >= chunks // 2, turn * (1 - 2 * (c // (chunks // 4) % 2)), 0)

        @pl.when(i == first_second)
        def _():
            loads[2].wait()
            loads[3].wait()

        @pl.when(stage == 0)
        def _():
            arrive(c)
            first(c)
            mid_start(c)

        @pl.when(stage == 1)
        def _():
            mid_wait(c)
            second(c)
            to_helper(c, right_out, got2, s3, r3).start()

        @pl.when(stage == 2)
        def _():
            to_helper(c, right_out, got2, s3, r3).wait_recv()
            third(c)
            for u in range(SPAN):
                step = c * SPAN + u

                @pl.when(step > 0)
                def _():
                    back_copy(step).start()

                @pl.when(step == 0)
                def _():
                    keep = pltpu.make_async_copy(delta.at[own], back.at[own], lsem.at[0])
                    keep.start()
                    keep.wait()

        return carry

    lax.fori_loop(0, len(plan), body, 0)
    rest = pl.ds(1, count - 1)
    others = pl.ds(cap, slots - cap)
    all_of(lab.at[rest], lsend.at[0])
    all_of(packed.at[others], send.at[0])
    all_of(mixed, s1.at[0])
    all_of(rank, s2.at[0])
    all_of(right_out, s3.at[0])
    all_of(delta.at[others], bsend.at[0])
    all_of(back.at[others], brecv.at[0])
    load_base.wait()


def finish_kernel(table, base, back, out, total, sem):
    requests, tiles, positions, _ = base.shape
    part = requests // PARTS
    saves = []
    for k in range(PARTS):
        for r in range(k * part, (k + 1) * part):
            added = back[table[1, r]].astype(F32).reshape(tiles, positions, LANES)
            total[r] = (base[r].astype(F32) + added).astype(BF)
        at = pl.ds(k * part, part)
        saves.append(pltpu.make_async_copy(total.at[at], out.at[at], sem.at[k]))
        saves[-1].start()
    for save in saves:
        save.wait()


VM = pl.BlockSpec(memory_space=pltpu.VMEM)
SM = pl.BlockSpec(memory_space=pltpu.SMEM)
ANY = pl.BlockSpec(memory_space=pl.ANY)
HBM = pl.BlockSpec(memory_space=pltpu.HBM)


def local(hidden_in, base_out, adapter_ids, left_blocks, right_blocks, down_rank, up_rank):
    servers = lax.axis_size("server")
    helpers = lax.axis_size("helper")
    requests, positions, width_here = hidden_in.shape
    adapters_here, blocks_here, flat = left_blocks.shape
    rank_width = down_rank.shape[2]
    tiles = width_here // LANES
    rows = positions * tiles
    wide = 2 * LANES
    slots = servers * CAP
    fits = (
        helpers == 2
        and BLOCK == LANES // 2
        and flat == BLOCK * BLOCK
        and blocks_here * helpers == BLOCK
        and 2 * tiles == blocks_here
        and positions == 4
        and rank_width * SUB == LANES
        and width_here == blocks_here * BLOCK
        and servers & (servers - 1) == 0
        and servers == 8 * SPAN
        and requests % PARTS == 0
        and max(requests, slots) <= LANES
    )
    if not fits:
        return plain(
            hidden_in, base_out, adapter_ids, left_blocks, right_blocks, down_rank, up_rank
        )

    def tiled(array):
        split_rows = array.reshape(requests, positions, tiles, LANES)
        return split_rows.transpose(0, 2, 1, 3)

    dma = pltpu.SemaphoreType.DMA
    by_slot = pltpu.VMEM((slots, rows, LANES), BF)
    chunks = servers // SPAN
    piece = pltpu.VMEM((slots, tiles, wide), BF)
    pieces = pltpu.VMEM((helpers, slots, tiles, wide), BF)
    down = jnp.swapaxes(down_rank, 1, 2)
    labels = (servers, 1, LANES)
    hidden = tiled(hidden_in)
    back, base, table = pl.pallas_call(
        functools.partial(fused_kernel, helpers, servers, adapters_here),
        out_shape=(
            pltpu.VMEM((slots, rows, LANES), BF),
            pltpu.VMEM(hidden.shape, BF),
            pltpu.SMEM((SUB, LANES), I32),
        ),
        in_specs=[HBM] * 7,
        out_specs=(ANY, ANY, SM),
        scratch_shapes=[
            pltpu.VMEM(left_blocks.shape, BF),
            pltpu.VMEM(right_blocks.shape, BF),
            pltpu.VMEM(down.shape, BF),
            pltpu.VMEM(up_rank.shape, BF),
            pltpu.VMEM((1, requests), I32),
            pltpu.VMEM((requests, tiles, positions, LANES), BF),
            by_slot,
            by_slot,
            pltpu.VMEM((SUB, LANES), I32),
            pltpu.VMEM(labels, I32),
            pltpu.VMEM(labels, I32),
            piece,
            pieces,
            pltpu.VMEM((slots // 2, SUB, LANES), F32),
            pltpu.VMEM((helpers, slots // 2, SUB, LANES), F32),
            piece,
            pieces,
            by_slot,
            by_slot,
            pltpu.VMEM((SPAN * CAP, rows, LANES), F32),
            pltpu.VMEM((wide, wide), BF),
            pltpu.VMEM((wide, wide), BF),
            dma((4,)),
            dma((3,)),
            dma((1,)),
            dma((1,)),
        ]
        + [dma((1,)), dma((chunks,))] * 5
        + [dma((1,))] * 2,
        compiler_params=pltpu.CompilerParams(
            collective_id=0, has_side_effects=True, vmem_limit_bytes=VMEM_LIMIT
        ),
        name="fused",
    )(
        *[
            pltpu.with_memory_space_constraint(x, pltpu.HBM)
            for x in (
                adapter_ids.reshape(1, requests),
                hidden,
                tiled(base_out),
                left_blocks,
                right_blocks,
                down,
                up_rank,
            )
        ]
    )
    out = pl.pallas_call(
        finish_kernel,
        out_shape=jax.ShapeDtypeStruct((requests, tiles, positions, LANES), BF),
        in_specs=[SM, VM, VM],
        out_specs=HBM,
        scratch_shapes=[pltpu.VMEM(hidden.shape, BF), dma((PARTS,))],
        name="finish",
    )(
        pltpu.with_memory_space_constraint(table, pltpu.SMEM),
        pltpu.with_memory_space_constraint(base, pltpu.VMEM),
        pltpu.with_memory_space_constraint(back, pltpu.VMEM),
    )
    return out.transpose(0, 2, 1, 3).reshape(requests, positions, width_here)


def solution(mesh):
    in_specs = (
        P("server", None, "helper"),
        P("server", None, "helper"),
        P("server"),
        P("server", "helper", None),
        P("server", "helper", None),
        P("server", "helper", None),
        P("server", None, "helper"),
    )
    out_specs = P("server", None, "helper")
    return jax.shard_map(local, mesh=mesh, in_specs=in_specs, out_specs=out_specs, check_vma=False)
```

```python
import functools

import jax
import jax.numpy as jnp
from jax import lax
from jax.experimental import pallas as pl
from jax.experimental.pallas import tpu as pltpu
from jax.sharding import PartitionSpec as P

BLOCK = 64
CAP = 2


def plain(hidden_in, base_out, adapter_ids, left_blocks, right_blocks, down_rank, up_rank):
    servers = lax.axis_size("server")
    requests, positions, width_here = hidden_in.shape
    adapters_here = left_blocks.shape[0]
    blocks_here = left_blocks.shape[1]
    block_size = BLOCK
    rank_width = down_rank.shape[2]
    slot_total = servers * CAP
    owners = adapter_ids // adapters_here
    local_id = adapter_ids % adapters_here
    number = jnp.arange(requests)
    earlier = (owners[:, None] == owners[None, :]) & (number[None, :] < number[:, None])
    target = owners * CAP + jnp.sum(earlier.astype(jnp.int32), axis=1)
    placing = (jnp.arange(slot_total)[:, None] == target[None, :]).astype(jnp.bfloat16)
    packed = jnp.dot(
        placing,
        hidden_in.reshape(requests, positions * width_here),
        preferred_element_type=jnp.float32,
    ).astype(jnp.bfloat16)
    labels = jnp.dot(
        placing, (local_id + 1).astype(jnp.bfloat16), preferred_element_type=jnp.float32
    ).astype(jnp.bfloat16)
    arrived, arrived_labels = (
        lax.all_to_all(
            packed.reshape(servers, CAP, positions, width_here),
            "server",
            split_axis=0,
            concat_axis=0,
            tiled=True,
        ),
        lax.all_to_all(
            labels.reshape(servers, CAP), "server", split_axis=0, concat_axis=0, tiled=True
        ),
    )
    row_count = slot_total * positions
    flat_rows = arrived.reshape(row_count, width_here)
    block_rows = arrived.reshape(row_count, blocks_here, block_size)
    slot_labels = arrived_labels.reshape(slot_total, 1).astype(jnp.int32)
    row_labels = jnp.broadcast_to(slot_labels, (slot_total, positions)).reshape(row_count)
    numbers = jnp.arange(adapters_here, dtype=jnp.int32)

    def first_factor(carry, inputs):
        mixed_acc, rank_acc = carry
        left_flat, down_tile, number = inputs
        left_tile = left_flat.reshape(blocks_here, block_size, block_size)
        selected = row_labels == number + 1
        mixed = jnp.einsum(
            "rij,ikj->rik", block_rows, left_tile, preferred_element_type=jnp.float32
        ).astype(jnp.bfloat16)
        mixed_acc = jnp.where(selected[:, None, None], mixed, mixed_acc)
        partial_rank = jnp.dot(flat_rows, down_tile, preferred_element_type=jnp.float32)
        rank_acc = jnp.where(selected[:, None], partial_rank, rank_acc)
        return ((mixed_acc, rank_acc), None)

    start_mixed = jnp.zeros((row_count, blocks_here, block_size), jnp.bfloat16)
    start_rank = jnp.zeros((row_count, rank_width), jnp.float32)
    (mixed_rows, rank_partial), ignored = lax.scan(
        first_factor, (start_mixed, start_rank), (left_blocks, down_rank, numbers)
    )
    turned = lax.all_to_all(mixed_rows, "helper", split_axis=2, concat_axis=1, tiled=True)
    rank_sum = lax.psum(rank_partial, "helper")
    rank_proj = rank_sum.astype(jnp.bfloat16)
    columns_here = turned.shape[2]

    def second_factor(carry, inputs):
        right_acc, low_acc = carry
        right_flat, up_tile, number = inputs
        right_tile = right_flat.reshape(right_flat.shape[0], block_size, block_size)
        selected = row_labels == number + 1
        right_out = jnp.einsum(
            "rik,kmi->rmk", turned, right_tile, preferred_element_type=jnp.float32
        ).astype(jnp.bfloat16)
        right_acc = jnp.where(selected[:, None, None], right_out, right_acc)
        low_out = jnp.dot(rank_proj, up_tile, preferred_element_type=jnp.float32).astype(
            jnp.bfloat16
        )
        low_acc = jnp.where(selected[:, None], low_out, low_acc)
        return ((right_acc, low_acc), None)

    start_right = jnp.zeros((row_count, block_size, columns_here), jnp.bfloat16)
    start_low = jnp.zeros((row_count, width_here), jnp.bfloat16)
    (right_rows, rank_rows), ignored = lax.scan(
        second_factor, (start_right, start_low), (right_blocks, up_rank, numbers)
    )
    monarch_rows = lax.all_to_all(
        right_rows, "helper", split_axis=1, concat_axis=2, tiled=True
    ).reshape(row_count, width_here)
    summed_rows = (monarch_rows.astype(jnp.float32) + rank_rows.astype(jnp.float32)).astype(
        jnp.bfloat16
    )
    back_delta = lax.all_to_all(
        summed_rows.reshape(servers, CAP, positions, width_here),
        "server",
        split_axis=0,
        concat_axis=0,
        tiled=True,
    )
    flat_buffer = back_delta.reshape(slot_total, -1)
    delta = (
        jnp.einsum("sr,sc->rc", placing, flat_buffer, preferred_element_type=jnp.float32)
        .astype(jnp.bfloat16)
        .reshape(requests, positions, width_here)
    )
    total = base_out.astype(jnp.float32) + delta.astype(jnp.float32)
    return total.astype(jnp.bfloat16)


LANES = 128
SUB = 8
SPAN = 2
VMEM_LIMIT = 56 << 20
PARTS = 4
PLAN = (
    ["F0", "F1", "FA", "S0", "S1", "FB", "SA", "F2"]
    + ["FC", "SB", "TA", "F3", "S2", "T0", "FD", "SC"]
    + ["TB", "T2", "S3", "SD", "T1", "TC", "T3", "TD"]
)
MESH = pl.DeviceIdType.MESH
NT = (((1,), (1,)), ((), ()))
BF = jnp.bfloat16
F32 = jnp.float32
I32 = jnp.int32


def iota(shape, dim=1):
    return lax.broadcasted_iota(I32, shape, dim)


def flipped(index, mask):
    other = index
    bit = 1
    while bit <= mask:
        if mask & bit:
            other = other + bit * (1 - 2 * lax.rem(lax.div(index, bit), 2))
        bit *= 2
    return other


def flipped_by(index, mask, count):
    other = index
    bit = 1
    while bit < count:
        has = lax.rem(lax.div(mask, bit), 2)
        other = other + bit * has * (1 - 2 * lax.rem(lax.div(index, bit), 2))
        bit *= 2
    return other


def plan_of(chunks):
    half, quarter = chunks // 2, chunks // 4
    named = dict(zip("0123", range(half)))
    named.update(zip("ABCD", [*range(half + quarter, chunks), *range(half, half + quarter)]))
    return [("FST".index(word[0]), named[word[1]]) for word in PLAN]


def pick(i, listed):
    value = jnp.asarray(listed[0], I32)
    for at, c in enumerate(listed[1:]):
        value = jnp.where(i == at + 1, jnp.asarray(c, I32), value)
    return value


def expand(x):
    low = iota(x.shape) < LANES // 2
    zero = jnp.zeros_like(x)
    turned = pltpu.roll(x, LANES // 2, 1)
    both = jnp.concatenate(
        [
            jnp.where(low, x, zero),
            jnp.where(low, turned, zero),
            jnp.where(low, zero, turned),
            jnp.where(low, zero, x),
        ],
        axis=0,
    )
    none = jnp.zeros_like(both)
    return jnp.concatenate(
        [jnp.concatenate([both, none], axis=1), jnp.concatenate([none, both], axis=1)], axis=0
    )


def diagonal(full, number):
    wide = full.shape[1]
    groups = full.shape[0] // (2 * SUB)
    sub = iota((SUB, wide), 0)
    parts = full.reshape(groups, 2, SUB, wide)
    upper = number >= SUB
    sets = []
    for h in range(groups // SUB):
        held = [
            jnp.where(upper, parts[h * SUB + c, 1], parts[h * SUB + c, 0]) for c in range(SUB)
        ]
        for bit in (4, 2, 1):
            here = (sub & bit) > 0
            same = ((number & bit) > 0) == here
            merged = []
            for c in range(bit):
                a, b = held[c], held[c + bit]
                kept = jnp.where(here, b, a)
                moved = jnp.where(here, a, b)
                if 2 * bit == SUB:
                    moved = pltpu.roll(moved, bit, 0)
                else:
                    moved = jnp.where(
                        here, pltpu.roll(moved, bit, 0), pltpu.roll(moved, SUB - bit, 0)
                    )
                merged.append(jnp.where(same, kept, moved))
            held = merged
        sets.append(held[0])
    return sets


def factor(w, which, groups, number, wide):
    chunks = w.shape[2] // wide
    sets = []
    for g, x in enumerate(groups):
        rows = jnp.concatenate(
            [
                w[which, 2 * SUB * g : 2 * SUB * (g + 1), c * wide : (c + 1) * wide]
                for c in range(chunks)
            ],
            axis=0,
        )
        full = lax.dot_general(rows, expand(x), NT, preferred_element_type=F32)
        sets.append(diagonal(full, number))
    return jnp.concatenate([sets[g][h] for h in range(2) for g in range(2)], axis=0)


def exchanged(ref, slot):
    first = (iota((SUB, LANES)) & 16) > 0
    second = (iota((2 * SUB, LANES)) & 32) > 0
    result = [[None, None] for _ in range(4)]
    for high in range(2):
        at = slice(high * LANES, (high + 1) * LANES)
        a, b = ref[0, slot, :, at], ref[1, slot, :, at]
        by_p = (
            jnp.where(second, pltpu.roll(b, 32, 1), a),
            jnp.where(second, b, pltpu.roll(a, LANES - 32, 1)),
        )
        for p1 in range(2):
            both = by_p[p1].astype(F32)
            a, b = both[:SUB], both[SUB:]
            result[2 * p1][high] = jnp.where(first, pltpu.roll(b, 16, 1), a)
            result[2 * p1 + 1][high] = jnp.where(first, b, pltpu.roll(a, LANES - 16, 1))
    return result


def stacked(ref, at, width):
    return jnp.concatenate(
        [ref[at, :, k * LANES : (k + 1) * LANES] for k in range(width // LANES)], axis=0
    )


def fused_kernel(
    helpers, count, adapters,
    ids_any, hid_any, base_any, left_any, right_any, down_any, up_any,
    back, base, table_s,
    left, right, down, up, ids, hid, packed, arrived, table, lab, lab_in,
    mixed, got1, rank, got_rank, right_out, got2, low, delta, order_m, perm1, perm2,
    wsem, isem, tsem, lsem, send, recv, lsend, lrecv, s1, r1, s2, r2, s3, r3, bsend, brecv,
):
    me = lax.axis_index("helper")
    here = lax.axis_index("server")
    other = 1 - me
    slots, rows, _ = packed.shape
    wide = mixed.shape[2]
    positions = 4
    tiles = rows // positions
    cap = slots // count
    chunks = count // SPAN
    size = SPAN * cap
    requests = ids.shape[1]

    barrier = pltpu.get_barrier_semaphore()
    for step in range(1, count):
        pl.semaphore_signal(
            barrier, inc=1, device_id={"server": flipped(here, step)}, device_id_type=MESH
        )
    pl.semaphore_signal(barrier, inc=1, device_id={"helper": other}, device_id_type=MESH)
    load_ids = pltpu.make_async_copy(ids_any, ids, isem.at[0])
    load_ids.start()
    load_hid = pltpu.make_async_copy(hid_any, hid, isem.at[1])
    load_hid.start()
    loads = [
        pltpu.make_async_copy(a, b, wsem.at[i])
        for i, (a, b) in enumerate(
            ((left_any, left), (down_any, down), (right_any, right), (up_any, up))
        )
    ]
    load_base = pltpu.make_async_copy(base_any, base, isem.at[2])

    load_ids.wait()
    loads[0].start()
    loads[1].start()
    names = ids[...]
    owner = jnp.zeros_like(names)
    for s in range(1, count):
        owner = owner + (names >= s * adapters).astype(I32)
    local = names - owner * adapters
    lane = iota((requests, requests))
    row = iota((requests, requests), 0)

    def column(line):
        return jnp.sum(jnp.where(lane == row, line, 0), axis=1, keepdims=True)

    owner_column = column(owner)
    same_owner = owner_column == owner
    before_line = jnp.sum((same_owner & (row < lane)).astype(I32), axis=0, keepdims=True)
    target_line = (owner ^ here) * cap + before_line
    target_column = column(target_line)
    slot_lane = iota((requests, LANES))
    hit = target_column == slot_lane
    inv_line = jnp.sum(jnp.where(hit, iota((requests, LANES), 0), 0), axis=0, keepdims=True)
    table[...] = jnp.zeros_like(table)
    table[0:1, :] = inv_line
    table[1:2, 0:requests] = target_line
    save = pltpu.make_async_copy(table, table_s, tsem.at[0])
    save.start()
    step_row = iota((count, requests), 0)
    step_line = owner ^ here
    lab_lane = iota((count, LANES))
    labels = jnp.zeros((count, LANES), I32)
    for u in range(cap):
        mine = (step_line == step_row) & (before_line == u)
        found = jnp.sum(jnp.where(mine, local, 0), axis=1, keepdims=True)
        labels = labels + jnp.where(lab_lane == u, found, 0)
    for step in range(count):
        lab[step] = labels[step : step + 1]
    lab_in[0] = labels[0:1]
    pl.semaphore_wait(barrier, count)

    def lab_copy(step):
        return pltpu.make_async_remote_copy(
            src_ref=lab.at[step], dst_ref=lab_in.at[step],
            send_sem=lsend.at[0], recv_sem=lrecv.at[step // SPAN],
            device_id={"server": flipped_by(here, step, count)}, device_id_type=MESH,
        )

    def data_copy(step):
        at = pl.ds(step * cap, cap)
        return pltpu.make_async_remote_copy(
            src_ref=packed.at[at], dst_ref=arrived.at[at],
            send_sem=send.at[0], recv_sem=recv.at[step // SPAN],
            device_id={"server": flipped_by(here, step, count)}, device_id_type=MESH,
        )

    def back_copy(step):
        at = pl.ds(step * cap, cap)
        return pltpu.make_async_remote_copy(
            src_ref=delta.at[at], dst_ref=back.at[at],
            send_sem=bsend.at[0], recv_sem=brecv.at[0],
            device_id={"server": flipped_by(here, step, count)}, device_id_type=MESH,
        )

    def to_helper(c, src, dst, s, r, scale=1):
        at = pl.ds(c * (size // scale), size // scale)
        return pltpu.make_async_remote_copy(
            src_ref=src.at[at], dst_ref=dst.at[me, at],
            send_sem=s.at[0], recv_sem=r.at[c],
            device_id={"helper": other}, device_id_type=MESH,
        )

    for step in range(1, count):
        lab_copy(step).start()
    save.wait()
    load_hid.wait()
    for s in range(slots):
        packed[s] = hid[table_s[0, s]].astype(F32).reshape(rows, LANES).astype(BF)
    issue = list(range(1, count // 4))
    for j in range(0, count // 4, SPAN):
        issue += [s + j + u for s in (3 * (count // 4), count // 2) for u in range(SPAN)]
    issue += list(range(count // 4, count // 2))
    for step in issue:
        data_copy(step).start()
    own = pl.ds(0, cap)
    arrived[own] = packed[own]

    src = iota((wide, wide), 0)
    dst = iota((wide, wide))
    q, low32, par = src & 192, src & 31, (src >> 5) & 1
    perm1[...] = (
        (q + (low32 & 3) * 16 + 2 * (low32 >> 2) + par == dst).astype(F32).astype(BF)
    )
    perm2[...] = (
        (q + (low32 >> 3) * 16 + 4 * (low32 & 3) + (low32 & 4) // 2 + par == dst)
        .astype(F32)
        .astype(BF)
    )
    code = iota((SUB, wide))
    low32, par = code & 31, (code >> 5) & 1
    number1 = 2 * (low32 >> 2) + par
    number2 = 4 * (low32 & 3) + (low32 & 4) // 2 + par
    sub = iota((SUB, LANES), 0)
    line = iota((SUB, LANES))
    top = sub < positions
    rank_width = LANES // SUB
    nothing = jnp.zeros((SUB, LANES), F32)

    def diag_of(b):
        return line // rank_width == 2 * (b % (tiles // 4)) + sub // positions

    def names_of(c):
        found = []
        for u in range(SPAN):
            line_of = lab_in[c * SPAN + u]
            found += [line_of[0, j] for j in range(cap)]
        return found

    def first(c):
        named = names_of(c)
        pieces, ranks = [], []
        for j in range(size):
            slot = c * size + j
            which = named[j]
            x = arrived[slot]
            pieces.append(factor(left, which, [x[: rows // 2], x[rows // 2 :]], number1, wide))
            part = lax.dot_general(
                x, stacked(down, which, tiles * LANES), NT, preferred_element_type=F32
            )
            total = None
            for b in range(rows // SUB):
                half = b // (tiles // 4)
                block = part[b * SUB : (b + 1) * SUB, half * LANES : (half + 1) * LANES]
                block = jnp.where(diag_of(b), block, 0.0)
                total = block if total is None else total + block
            ranks.append(total + pltpu.roll(total, positions, 0))
        turned = jnp.dot(
            jnp.concatenate(pieces, axis=0).astype(BF), perm1[...], preferred_element_type=F32
        ).astype(BF)
        for j in range(size):
            slot = c * size + j
            a = turned[j * 2 * tiles : j * 2 * tiles + tiles]
            b = turned[j * 2 * tiles + tiles : (j + 1) * 2 * tiles]
            got1[me, slot] = jnp.where(me == 0, a, b)
            mixed[slot] = jnp.where(me == 0, b, a)
        for k in range(size // 2):
            pair = c * (size // 2) + k
            both = jnp.where(top, ranks[2 * k], ranks[2 * k + 1])
            rank[pair] = both
            got_rank[me, pair] = both

    def second(c):
        named = names_of(c)
        pieces = []
        for k in range(size // 2):
            pair = c * (size // 2) + k
            total = got_rank[0, pair] + got_rank[1, pair]
            for shift in (64, 32, 16):
                total = total + pltpu.roll(total, shift, 1)
            total = total.astype(BF).astype(F32)
            swapped = pltpu.roll(total, positions, 0)
            for u in range(2):
                slot = c * size + 2 * k + u
                which = named[2 * k + u]
                held = exchanged(got1, slot)
                groups = []
                for g in range(2):
                    blocks = []
                    for p in range(positions):
                        a, b = held[p]
                        if g == 0:
                            blocks.append(jnp.where(top, a, pltpu.roll(b, positions, 0)))
                        else:
                            blocks.append(jnp.where(top, pltpu.roll(a, positions, 0), b))
                    groups.append(jnp.concatenate(blocks, axis=0).astype(BF))
                pieces.append(factor(right, which, groups, number2, wide))
                mine = jnp.where(top, total, swapped) if u == 0 else jnp.where(top, swapped, total)
                blocks = []
                for b in range(rows // SUB):
                    kept = jnp.where(diag_of(b), mine, 0.0)
                    pair_of = [kept, nothing] if b < rows // SUB // 2 else [nothing, kept]
                    blocks.append(jnp.concatenate(pair_of, axis=1))
                tall = jnp.concatenate(blocks, axis=0).astype(BF)
                low[slot] = jnp.dot(
                    tall, stacked(up, which, tiles * LANES), preferred_element_type=F32
                ).astype(BF)
        turned = jnp.dot(
            jnp.concatenate(pieces, axis=0).astype(BF), perm2[...], preferred_element_type=F32
        ).astype(BF)
        for j in range(size):
            slot = c * size + j
            a = turned[j * 2 * tiles : j * 2 * tiles + tiles]
            b = turned[j * 2 * tiles + tiles : (j + 1) * 2 * tiles]
            got2[me, slot] = jnp.where(me == 0, a, b)
            right_out[slot] = jnp.where(me == 0, b, a)

    def third(c):
        for j in range(size):
            slot = c * size + j
            held = exchanged(got2, slot)
            for p in range(positions):
                for high in range(2):
                    order_m[j, pl.ds(positions * high + p, SUB, stride=SUB), :] = held[p][high]
        for j in range(size):
            slot = c * size + j
            delta[slot] = (order_m[j] + low[slot].astype(F32)).astype(BF)

    loads[0].wait()
    loads[1].wait()
    loads[2].start()
    loads[3].start()
    load_base.start()

    def all_of(ref, sem):
        pltpu.make_async_copy(ref, ref, sem).wait()

    def arrive(c):
        @pl.when(c == 0)
        def _():
            all_of(lab_in.at[pl.ds(1, SPAN - 1)], lrecv.at[0])
            all_of(arrived.at[pl.ds(cap, (SPAN - 1) * cap)], recv.at[0])

        @pl.when(c > 0)
        def _():
            all_of(lab_in.at[pl.ds(c * SPAN, SPAN)], lrecv.at[c])
            all_of(arrived.at[pl.ds(c * size, size)], recv.at[c])

    def mid_wait(c):
        to_helper(c, mixed, got1, s1, r1).wait_recv()
        to_helper(c, rank, got_rank, s2, r2, 2).wait_recv()

    def mid_start(c):
        to_helper(c, mixed, got1, s1, r1).start()
        to_helper(c, rank, got_rank, s2, r2, 2).start()

    plan = plan_of(chunks)
    quarter = count // 4
    inner = lax.rem(lax.div(here, quarter), 2) != lax.div(here, 2 * quarter)
    turn = jnp.where(inner, chunks // 4, 0)
    first_second = [stage for stage, _ in plan].index(1)

    def turned_of(c):
        return c + turn * (1 - 2 * (c // (chunks // 4) % 2)) if c >= chunks // 2 else c

    def body(i, carry):
        code = pick(i, [stage * chunks + c for stage, c in plan])
        stage, c = code // chunks, code % chunks
        c = c + jnp.where(c >= chunks // 2, turn * (1 - 2 * (c // (chunks // 4) % 2)), 0)

        @pl.when(i == first_second)
        def _():
            loads[2].wait()
            loads[3].wait()

        @pl.when(stage == 0)
        def _():
            arrive(c)
            first(c)
            mid_start(c)

        @pl.when(stage == 1)
        def _():
            mid_wait(c)
            second(c)
            to_helper(c, right_out, got2, s3, r3).start()

        @pl.when(stage == 2)
        def _():
            to_helper(c, right_out, got2, s3, r3).wait_recv()
            third(c)
            for u in range(SPAN):
                step = c * SPAN + u

                @pl.when(step > 0)
                def _():
                    back_copy(step).start()

                @pl.when(step == 0)
                def _():
                    keep = pltpu.make_async_copy(delta.at[own], back.at[own], lsem.at[0])
                    keep.start()
                    keep.wait()

        return carry

    lax.fori_loop(0, len(plan), body, 0)
    rest = pl.ds(1, count - 1)
    others = pl.ds(cap, slots - cap)
    all_of(lab.at[rest], lsend.at[0])
    all_of(packed.at[others], send.at[0])
    all_of(mixed, s1.at[0])
    all_of(rank, s2.at[0])
    all_of(right_out, s3.at[0])
    all_of(delta.at[others], bsend.at[0])
    all_of(back.at[others], brecv.at[0])
    load_base.wait()


def finish_kernel(table, base, back, out, total, sem):
    requests, tiles, positions, _ = base.shape
    part = requests // PARTS
    saves = []
    for k in range(PARTS):
        for r in range(k * part, (k + 1) * part):
            added = back[table[1, r]].astype(F32).reshape(tiles, positions, LANES)
            total[r] = (base[r].astype(F32) + added).astype(BF)
        at = pl.ds(k * part, part)
        saves.append(pltpu.make_async_copy(total.at[at], out.at[at], sem.at[k]))
        saves[-1].start()
    for save in saves:
        save.wait()


VM = pl.BlockSpec(memory_space=pltpu.VMEM)
SM = pl.BlockSpec(memory_space=pltpu.SMEM)
ANY = pl.BlockSpec(memory_space=pl.ANY)
HBM = pl.BlockSpec(memory_space=pltpu.HBM)


def local(hidden_in, base_out, adapter_ids, left_blocks, right_blocks, down_rank, up_rank):
    servers = lax.axis_size("server")
    helpers = lax.axis_size("helper")
    requests, positions, width_here = hidden_in.shape
    adapters_here, blocks_here, flat = left_blocks.shape
    rank_width = down_rank.shape[2]
    tiles = width_here // LANES
    rows = positions * tiles
    wide = 2 * LANES
    slots = servers * CAP
    fits = (
        helpers == 2
        and BLOCK == LANES // 2
        and flat == BLOCK * BLOCK
        and blocks_here * helpers == BLOCK
        and 2 * tiles == blocks_here
        and positions == 4
        and rank_width * SUB == LANES
        and width_here == blocks_here * BLOCK
        and servers & (servers - 1) == 0
        and servers == 8 * SPAN
        and requests % PARTS == 0
        and max(requests, slots) <= LANES
    )
    if not fits:
        return plain(
            hidden_in, base_out, adapter_ids, left_blocks, right_blocks, down_rank, up_rank
        )

    def tiled(array):
        split_rows = array.reshape(requests, positions, tiles, LANES)
        return split_rows.transpose(0, 2, 1, 3)

    dma = pltpu.SemaphoreType.DMA
    by_slot = pltpu.VMEM((slots, rows, LANES), BF)
    chunks = servers // SPAN
    piece = pltpu.VMEM((slots, tiles, wide), BF)
    pieces = pltpu.VMEM((helpers, slots, tiles, wide), BF)
    down = jnp.swapaxes(down_rank, 1, 2)
    labels = (servers, 1, LANES)
    hidden = tiled(hidden_in)
    back, base, table = pl.pallas_call(
        functools.partial(fused_kernel, helpers, servers, adapters_here),
        out_shape=(
            pltpu.VMEM((slots, rows, LANES), BF),
            pltpu.VMEM(hidden.shape, BF),
            pltpu.SMEM((SUB, LANES), I32),
        ),
        in_specs=[HBM] * 7,
        out_specs=(ANY, ANY, SM),
        scratch_shapes=[
            pltpu.VMEM(left_blocks.shape, BF),
            pltpu.VMEM(right_blocks.shape, BF),
            pltpu.VMEM(down.shape, BF),
            pltpu.VMEM(up_rank.shape, BF),
            pltpu.VMEM((1, requests), I32),
            pltpu.VMEM((requests, tiles, positions, LANES), BF),
            by_slot,
            by_slot,
            pltpu.VMEM((SUB, LANES), I32),
            pltpu.VMEM(labels, I32),
            pltpu.VMEM(labels, I32),
            piece,
            pieces,
            pltpu.VMEM((slots // 2, SUB, LANES), F32),
            pltpu.VMEM((helpers, slots // 2, SUB, LANES), F32),
            piece,
            pieces,
            by_slot,
            by_slot,
            pltpu.VMEM((SPAN * CAP, rows, LANES), F32),
            pltpu.VMEM((wide, wide), BF),
            pltpu.VMEM((wide, wide), BF),
            dma((4,)),
            dma((3,)),
            dma((1,)),
            dma((1,)),
        ]
        + [dma((1,)), dma((chunks,))] * 5
        + [dma((1,))] * 2,
        compiler_params=pltpu.CompilerParams(
            collective_id=0, has_side_effects=True, vmem_limit_bytes=VMEM_LIMIT
        ),
        name="fused",
    )(
        *[
            pltpu.with_memory_space_constraint(x, pltpu.HBM)
            for x in (
                adapter_ids.reshape(1, requests),
                hidden,
                tiled(base_out),
                left_blocks,
                right_blocks,
                down,
                up_rank,
            )
        ]
    )
    out = pl.pallas_call(
        finish_kernel,
        out_shape=jax.ShapeDtypeStruct((requests, tiles, positions, LANES), BF),
        in_specs=[SM, VM, VM],
        out_specs=HBM,
        scratch_shapes=[pltpu.VMEM(hidden.shape, BF), dma((PARTS,))],
        name="finish",
    )(
        pltpu.with_memory_space_constraint(table, pltpu.SMEM),
        pltpu.with_memory_space_constraint(base, pltpu.VMEM),
        pltpu.with_memory_space_constraint(back, pltpu.VMEM),
    )
    return out.transpose(0, 2, 1, 3).reshape(requests, positions, width_here)


def solution(mesh):
    in_specs = (
        P("server", None, "helper"),
        P("server", None, "helper"),
        P("server"),
        P("server", "helper", None),
        P("server", "helper", None),
        P("server", "helper", None),
        P("server", None, "helper"),
    )
    out_specs = P("server", None, "helper")
    return jax.shard_map(local, mesh=mesh, in_specs=in_specs, out_specs=out_specs, check_vma=False)
```
